512 devices in a mesh: freq: 8 (over z), sx: 16 (over y, core), sy: 4 (over x).
Axes of the slice: x: 4, y: 8, z: 8, core: 2. Of those that a mesh axis runs over, the one named last changes fastest.
Arguments:
- stiffness: bfloat16 [16, 4, 3072, 3072], P('sx', 'sy', None, 'freq'), as said below
- mass_matrix: bfloat16 [16, 4, 3072, 3072], P('sx', 'sy', None, 'freq'), as said below
- omega_table: float32 [32], replicated, may hold values from 0.5 to 6
- assignment: int32 [32], P('freq'), may hold values from 0 to 31, each once
- adjoint_load: float32 [16, 4, 32, 2, 4, 768], P('sx', 'sy', 'freq'), as said below
- forward_state: bfloat16 [16, 4, 32, 2, 4, 768], P('sx', 'sy', 'freq'), may hold values from -6 to 6
- owner_index: int32 [16, 4, 4, 768], P('sx', 'sy'), may hold values from 0 to 1727
Outputs:
- adjoint: float32 [16, 4, 32, 2, 4, 768], P('sx', 'sy', 'freq')
- gradient: float32 [16, 4, 1728], P('sx', 'sy', 'freq')
- residual_level: float32 [32], P('freq')
The draws below stay inside these ranges and needn't reach their ends.
Inputs may be any that keep to these rules, and one draw needn't show every extreme that they name: `stiffness`: each substructure's K, read as in the reference program, is symmetric. `mass_matrix`: each substructure's M, read as in the reference program, is symmetric. `adjoint_load`: the two copies of a face shared by neighbouring substructures are equal.
All inputs are finite; a program needn't handle non-finite values.
Results may differ from the reference program's by a relative error of at most 0.012.
Values may be sent and summed in bfloat16 or wider, within the bound.
No kernel may reach another device: no remote copies, remote signals or barrier semaphores. Data moves between devices by JAX's collectives and lax.ppermute only.
A program may use at most 64 MiB of HBM per device.

```python
import math
import jax
import jax.numpy as jnp
from jax import lax

NF = 768
NB = 3072
NFREQS = 32
ITERS = 4
DE_SUB = 1728
NSUBX = 16
NSUBY = 4


def symmetric_part(key, diagonal_value, spread):
    normal_draw = jax.random.normal(key, (NSUBX, NSUBY, NB, NB), jnp.float32)
    symmetric = (normal_draw + jnp.swapaxes(normal_draw, 2, 3)) * 0.5 ** 0.5
    identity = jnp.eye(NB, dtype=jnp.float32)
    matrix = diagonal_value * identity + spread / NB ** 0.5 * symmetric
    reordered = jnp.swapaxes(matrix.reshape(NSUBX, NSUBY, NB, 4, NF), 3, 4)
    return reordered.reshape(NSUBX, NSUBY, NB, 4 * NF).astype(jnp.bfloat16)


def draw_stiffness(key, part):
    return symmetric_part(jax.random.fold_in(key, 11), 4.0, 1.0)


def draw_mass_matrix(key, part):
    return symmetric_part(jax.random.fold_in(key, 23), 1.0, 0.25)


def face_values(key, count_x, count_y, shift_x):
    out_shape = (count_x, count_y, NFREQS, 2, NF)
    base_key = jax.random.fold_in(key, 5)
    level_key = jax.random.fold_in(key, 9)
    frac_x = (jnp.arange(count_x, dtype=jnp.float32) + shift_x) / NSUBX
    growth = (3.0 ** frac_x)[:, None, None, None, None]
    levels = jnp.exp(jax.random.uniform(level_key, out_shape, jnp.float32, 0.0, math.log(10.0)))
    base_draw = jax.random.normal(base_key, out_shape, jnp.float32)
    return 0.3 * base_draw * levels * growth


def draw_adjoint_load(key, part):
    faces_x = face_values(jax.random.fold_in(key, 31), NSUBX + 1, NSUBY, 0.0)
    faces_y = face_values(jax.random.fold_in(key, 37), NSUBX, NSUBY + 1, 0.5)
    return jnp.stack([faces_x[:-1], faces_x[1:], faces_y[:, :-1], faces_y[:, 1:]], axis=4)


def touch_ends(result, own_key, low, top_value):
    longest = result.shape.index(max(result.shape))
    spots = []
    for shift in (0, 1):
        where = [jax.random.randint(jax.random.fold_in(own_key, axis), (), 0, length) for axis, length in enumerate(result.shape)]
        where[longest] = (where[longest] + shift) % result.shape[longest]
        spots.append(tuple(where))
    return result.at[spots[0]].set(low).at[spots[1]].set(top_value)


def block_scale(key, dims, pieces, low, high):
    def one(axis_at, parts):
        steps = jax.random.uniform(jax.random.fold_in(jax.random.fold_in(key, 6), axis_at), (parts,), jnp.float32, low / len(pieces), high / len(pieces))
        return jnp.repeat(jnp.exp(steps), dims[axis_at] // parts).reshape((-1,) + (1,) * (len(dims) - axis_at - 1))

    gain = one(*pieces[0])
    for cut in pieces[1:]:
        gain = gain * one(*cut)
    return gain


def noise(key, shape, width, most, split=(), held_as=jnp.bfloat16):
    entries = width * jax.random.normal(key, shape, jnp.float32)
    if split:
        entries = entries * block_scale(key, shape, split, -0.22, 0.18)
    return jnp.clip(entries, -most, most).astype(held_as)


def setup_inputs(seed: int = 0) -> dict:
    key_list = jax.random.split(jax.random.key(seed), 8)
    stiffness = draw_stiffness(jax.random.fold_in(key_list[7], 71), 0)
    mass_matrix = draw_mass_matrix(jax.random.fold_in(key_list[7], 71), 0)
    omega_table = jnp.clip(jnp.exp(jax.random.uniform(key_list[2], (NFREQS,), jnp.float32, math.log(0.5), math.log(6.0))), 0.5, 6.0)
    assignment = jax.random.permutation(key_list[3], NFREQS).astype(jnp.int32)
    adjoint_load = draw_adjoint_load(jax.random.fold_in(key_list[7], 71), 0)
    forward_state = noise(key_list[5], (NSUBX, NSUBY, NFREQS, 2, 4, NF), 1.0, 6.0, ((0, 16), (1, 4), (2, 8)))
    owner_index = touch_ends(jax.random.randint(key_list[6], (NSUBX, NSUBY, 4, NF), 0, DE_SUB), jax.random.fold_in(key_list[6], 1), 0, DE_SUB - 1).astype(jnp.int32)
    return {"stiffness": stiffness, "mass_matrix": mass_matrix, "omega_table": omega_table, "assignment": assignment, "adjoint_load": adjoint_load, "forward_state": forward_state, "owner_index": owner_index}


LOSS_FACTOR = 0.3


def face_weights():
    index_x = jnp.arange(NSUBX, dtype=jnp.int32)[:, None] * jnp.ones((1, NSUBY), jnp.int32)
    index_y = jnp.ones((NSUBX, 1), jnp.int32) * jnp.arange(NSUBY, dtype=jnp.int32)[None, :]
    west_weight = jnp.where(index_x > 0, 0.5, 1.0)
    east_weight = jnp.where(index_x < NSUBX - 1, 0.5, 1.0)
    south_weight = jnp.where(index_y > 0, 0.5, 1.0)
    north_weight = jnp.where(index_y < NSUBY - 1, 0.5, 1.0)
    return jnp.stack([west_weight, east_weight, south_weight, north_weight], axis=-1).astype(jnp.float32)


def face_major(matrix):
    sub_count = NSUBX * NSUBY
    return jnp.swapaxes(matrix.reshape(sub_count, NB, NF, 4), 2, 3).reshape(sub_count, NB, NB)


def local_products(vector, stiffness, mass_matrix):
    sub_count = NSUBX * NSUBY
    stacked_rows = vector.astype(jnp.bfloat16).reshape(sub_count, NFREQS * 2, NB)
    stiff_flat = face_major(stiffness)
    mass_flat = face_major(mass_matrix)

    def per_substructure(packed):
        rows_in, stiff_one, mass_one = packed
        return (jnp.dot(rows_in, stiff_one, preferred_element_type=jnp.float32),
                jnp.dot(rows_in, mass_one, preferred_element_type=jnp.float32))

    stiff_part, mass_part = lax.map(per_substructure, (stacked_rows, stiff_flat, mass_flat))
    out_shape = (NSUBX, NSUBY, NFREQS, 2, 4, NF)
    return stiff_part.reshape(out_shape), mass_part.reshape(out_shape)


def assemble(local_vals):
    west_face = local_vals[:, :, :, :, 0]
    east_face = local_vals[:, :, :, :, 1]
    south_face = local_vals[:, :, :, :, 2]
    north_face = local_vals[:, :, :, :, 3]
    zero_row = jnp.zeros_like(west_face[:1])
    zero_col = jnp.zeros_like(south_face[:, :1])
    from_left = jnp.concatenate([zero_row, east_face[:-1]], axis=0)
    from_right = jnp.concatenate([west_face[1:], zero_row], axis=0)
    from_below = jnp.concatenate([zero_col, north_face[:, :-1]], axis=1)
    from_above = jnp.concatenate([south_face[:, 1:], zero_col], axis=1)
    return jnp.stack([west_face + from_left, east_face + from_right,
                      south_face + from_below, north_face + from_above], axis=4)


def operate(vector, stiffness, mass_matrix, omega_sq, sign_factor):
    stiff_part, mass_part = local_products(vector, stiffness, mass_matrix)
    factor = omega_sq[None, None, :, None, None]
    real_part = stiff_part[:, :, :, 0] - sign_factor * LOSS_FACTOR * stiff_part[:, :, :, 1] - factor * mass_part[:, :, :, 0]
    imag_part = stiff_part[:, :, :, 1] + sign_factor * LOSS_FACTOR * stiff_part[:, :, :, 0] - factor * mass_part[:, :, :, 1]
    return assemble(jnp.stack([real_part, imag_part], axis=3))


def inner(first_vec, second_vec, weights):
    return jnp.sum(first_vec * second_vec * weights[:, :, None, None, :, None], axis=(0, 1, 3, 4, 5))


def per_freq(values):
    return values[None, None, :, None, None, None]


def reference(stiffness, mass_matrix, omega_table, assignment, adjoint_load, forward_state, owner_index):
    omega_sq = omega_table[assignment]
    weights = face_weights()
    residual = adjoint_load
    solution = jnp.zeros_like(adjoint_load)
    normal_res = operate(residual, stiffness, mass_matrix, omega_sq, -1.0)
    direction = normal_res
    gamma_now = inner(normal_res, normal_res, weights)
    for iteration in range(ITERS):
        image_vec = operate(direction, stiffness, mass_matrix, omega_sq, 1.0)
        delta_now = inner(image_vec, image_vec, weights)
        step_size = gamma_now / delta_now
        solution = solution + per_freq(step_size) * direction
        if iteration + 1 < ITERS:
            residual = residual - per_freq(step_size) * image_vec
            normal_res = operate(residual, stiffness, mass_matrix, omega_sq, -1.0)
            gamma_next = inner(normal_res, normal_res, weights)
            direction = normal_res + per_freq(gamma_next / gamma_now) * direction
            gamma_now = gamma_next
    residual_level = jnp.log(gamma_now / float(NSUBX * NSUBY * 2 * NB))
    state_vec = forward_state.astype(jnp.float32)
    lambda_real = solution[:, :, :, 0]
    lambda_imag = solution[:, :, :, 1]
    state_real = state_vec[:, :, :, 0]
    state_imag = state_vec[:, :, :, 1]
    product_term = (lambda_real * state_real - lambda_imag * state_imag) - LOSS_FACTOR * (lambda_real * state_imag + lambda_imag * state_real)
    dof_total = jnp.sum(product_term, axis=2)
    grad_factor = (DE_SUB / (NFREQS * NB)) ** 0.5

    def per_substructure(packed):
        values, owners = packed
        return jax.ops.segment_sum(values.reshape(-1), owners.reshape(-1), num_segments=DE_SUB)

    gradient = lax.map(per_substructure, (dof_total.reshape(NSUBX * NSUBY, 4, NF),
                                          owner_index.reshape(NSUBX * NSUBY, 4, NF)))
    gradient = -grad_factor * gradient.reshape(NSUBX, NSUBY, DE_SUB)
    return solution, gradient, residual_level
```

```python
import functools

import jax
import jax.numpy as jnp
from jax import lax
from jax.experimental import pallas as pl
from jax.experimental.pallas import tpu as pltpu
from jax.sharding import PartitionSpec as P

DE_SUB = 1728
LOSS_FACTOR = 0.3
LOW = 64
BF = jnp.bfloat16
F32 = jnp.float32


def params():
    return pltpu.CompilerParams(vmem_limit_bytes=24 * 1024 * 1024)


def arrange_kernel(stiff_ref, mass_ref, out_ref, order_ref):
    faces, _, run, width = stiff_ref.shape

    @pl.when(pl.program_id(0) == 0)
    def _():
        source = lax.broadcasted_iota(jnp.int32, (width, width), 0)
        target = lax.broadcasted_iota(jnp.int32, (width, width), 1)
        wanted = faces * lax.rem(target, run) + lax.div(target, run)
        order_ref[...] = jnp.where(source == wanted, 1.0, 0.0).astype(BF)

    for at, ref in enumerate((stiff_ref, mass_ref)):
        rows = ref[...].reshape(faces * run, width)
        moved = jnp.dot(rows, order_ref[...], preferred_element_type=F32)
        out_ref[0, :, at * width : (at + 1) * width] = moved.astype(BF)


def arrange(stiffness, mass_matrix, faces, n_freq):
    order, width = stiffness.shape
    run = order // (faces * n_freq)
    block = pl.BlockSpec((faces, 1, run, width), lambda d: (0, d, 0, 0))
    return pl.pallas_call(
        arrange_kernel,
        grid=(n_freq,),
        in_specs=[block, block],
        out_specs=pl.BlockSpec((1, width, 2 * width), lambda d: (d, 0, 0)),
        out_shape=jax.ShapeDtypeStruct((n_freq, width, 2 * width), BF),
        scratch_shapes=[pltpu.VMEM((width, width), BF)],
        compiler_params=params(),
        name="arrange",
    )(
        stiffness.reshape(faces, n_freq, run, width),
        mass_matrix.reshape(faces, n_freq, run, width),
    )


def apply_kernel(sign, faces, field_ref, pair_ref, omega_ref, local_ref, *rest):
    face_refs, sum_ref = rest[:faces], rest[faces]
    step = pl.program_id(0)
    width = local_ref.shape[1]
    rows = field_ref[...].reshape(-1, field_ref.shape[-1])
    count = rows.shape[0]
    if rows.dtype == F32:
        head = rows.astype(BF)
        rows = jnp.concatenate([head, (rows - head.astype(F32)).astype(BF)], axis=0)
    product = jnp.dot(rows, pair_ref[0], preferred_element_type=F32)
    if rows.shape[0] != count:
        product = product[:count] + product[count:]

    @pl.when(step == 0)
    def _():
        sum_ref[...] = product

    @pl.when(step > 0)
    def _():
        sum_ref[...] += product

    @pl.when(step == pl.num_programs(0) - 1)
    def _():
        stiff_part = sum_ref[:, :width]
        mass_part = sum_ref[:, width:]
        row = lax.broadcasted_iota(jnp.int32, (count, width), 0)
        real = lax.rem(row, 8) < 4
        other = jnp.where(
            real, -pltpu.roll(stiff_part, count - 4, 0), pltpu.roll(stiff_part, 4, 0)
        )
        local = stiff_part + (sign * LOSS_FACTOR) * other - omega_ref[...] * mass_part
        local_ref[...] = local
        run = width // faces
        for face, ref in enumerate(face_refs):
            ref[...] = local[:, face * run : (face + 1) * run]


def apply_local(field, pair, omega_rows, sign, faces, by_slot=False):
    n_freq, width, double = pair.shape
    count = omega_rows.shape[0]
    run = width // faces
    if by_slot:
        field_spec = pl.BlockSpec((n_freq, count // n_freq, width), lambda d: (0, 0, d))
    else:
        field_spec = pl.BlockSpec((1, count, width), lambda d: (d, 0, 0))
    whole = lambda d: (0, 0)
    return pl.pallas_call(
        functools.partial(apply_kernel, sign, faces),
        grid=(n_freq,),
        in_specs=[
            field_spec,
            pl.BlockSpec((1, width, double), lambda d: (d, 0, 0)),
            pl.BlockSpec((count, 1), whole),
        ],
        out_specs=[pl.BlockSpec((count, width), whole)]
        + [pl.BlockSpec((count, run), whole)] * faces,
        out_shape=[jax.ShapeDtypeStruct((count, width), F32)]
        + [jax.ShapeDtypeStruct((count, run), F32)] * faces,
        scratch_shapes=[pltpu.VMEM((count, double), F32)],
        compiler_params=params(),
        name="apply_local",
    )(field, pair, omega_rows)


def swap_faces(face_vals, once=False):
    west, east, south, north = face_vals

    def shift(values, axis, by):
        count = lax.axis_size(axis)
        pairs = [(i, i + by) for i in range(count) if 0 <= i + by < count]
        return lax.ppermute(values, axis, pairs)

    return (
        shift(east, "sx", 1),
        None if once else shift(west, "sx", -1),
        shift(north, "sy", 1),
        None if once else shift(south, "sy", -1),
    )


def finish_kernel(plan, faces, n_in, copies, *refs):
    combine, products, keep, send, places = plan
    given = sum(i is not None for i in places)
    local_ref, face_refs = refs[0], refs[1 : 1 + given]
    earlier = refs[1 + given : 1 + given + n_in]
    at = 1 + given + n_in
    coefs_ref = weight_ref = None
    if combine:
        coefs_ref, at = refs[at], at + 1
    if products:
        weight_ref, at = refs[at], at + 1
    outs = list(refs[at:])
    vector = local_ref[...]
    run = vector.shape[1] // faces
    halo = [jnp.zeros((vector.shape[0], run), F32) if i is None else face_refs[i][...] for i in places]
    vector = vector + jnp.concatenate(halo, axis=1)
    known = [ref[...] for ref in earlier]
    if combine:
        vector = vector * coefs_ref[:, len(combine) : len(combine) + 1]
        for slot, which in enumerate(combine):
            vector = vector + known[which] * coefs_ref[:, slot : slot + 1]
    known.append(vector)
    if keep:
        outs.pop(0)[...] = vector
    sums = None
    if products:
        weight = weight_ref[...]
        count = vector.shape[0]
        lane = lax.broadcasted_iota(jnp.int32, (count, 128), 1)
        sums = jnp.zeros((count, 128), F32)
        for slot, (left, right) in enumerate(products):
            value = jnp.sum(known[left] * known[right] * weight, axis=1, keepdims=True)
            sums = jnp.where(lane == slot, value, sums)
    if send is not None:
        sent = vector.astype(send)
        width = sent.shape[1]
        out = outs.pop(0)
        for copy in range(copies):
            out[copy, :, :width] = sent
            if products:
                out[copy, :, width:] = sums
    elif products:
        outs.pop(0)[...] = sums


def finish(
    local, halos, n_freq, earlier=(), combine=(), coefs=None, products=(), weight=None,
    keep=True, send=BF,
):
    count, width = local.shape
    given = [i for i, halo in enumerate(halos) if halo is not None]
    places = tuple(given.index(i) if i in given else None for i in range(len(halos)))
    args = [local, *(halos[i] for i in given), *earlier]
    if combine:
        args.append(coefs)
    if products:
        args.append(weight)
    shapes = []
    if keep:
        shapes.append(jax.ShapeDtypeStruct((count, width), F32))
    if send is not None:
        extra = 128 if products else 0
        shapes.append(jax.ShapeDtypeStruct((n_freq, count, width + extra), send))
    elif products:
        shapes.append(jax.ShapeDtypeStruct((count, 128), F32))
    plan = (tuple(combine), tuple(products), keep, send, places)
    return pl.pallas_call(
        functools.partial(finish_kernel, plan, len(halos), len(earlier), n_freq),
        out_shape=shapes,
        compiler_params=params(),
        name="finish",
    )(*args)


def exchange(blocks, axis):
    return lax.all_to_all(blocks, axis, 0, 0, tiled=False)


def total(values, axis):
    count = lax.axis_size(axis)
    return jnp.sum(exchange(jnp.broadcast_to(values[None], (count, *values.shape)), axis), axis=0)


def quad(entries, coefs):
    result = 0.0
    for i, left in enumerate(coefs):
        for j in range(i, len(coefs)):
            if left is None or coefs[j] is None:
                continue
            term = left * coefs[j] * entries[(i, j)]
            result = result + (term if i == j else 2.0 * term)
    return result


def combo(first, scale, second):
    out = []
    for a, b in zip(first, second):
        b = None if b is None else scale * b
        out.append(b if a is None else a if b is None else a + b)
    return out


def first_scalars(g, w):
    one = jnp.ones_like(g[(0, 0)])
    alpha0 = g[(0, 0)] / w[(0, 0)]
    res1 = [one, -alpha0]
    gamma1 = quad(g, res1)
    beta0 = gamma1 / g[(0, 0)]
    dir1 = [one + beta0, -alpha0]
    alpha1 = gamma1 / quad(w, dir1)
    return alpha0, res1, gamma1, beta0, dir1, alpha1


def last_scalars(g, w):
    alpha0, res1, gamma1, beta0, dir1, alpha1 = first_scalars(g, w)
    one = jnp.ones_like(alpha0)
    res1 = res1 + [None, None]
    dir1 = dir1 + [None, None]
    res2 = [None, None, one, None]
    gamma2 = g[(2, 2)]
    beta1 = gamma2 / gamma1
    dir2 = combo(res2, beta1, dir1)
    alpha2 = gamma2 / quad(w, dir2)
    change = combo(res1, -1.0, res2)
    image = combo([None, None, None, one], beta1 / alpha1, change)
    res3 = combo(res2, -alpha2, image)
    gamma3 = quad(g, res3)
    dir3 = combo(res3, gamma3 / gamma2, dir2)
    alpha3 = gamma3 / quad(w, dir3)
    answer = combo([alpha0, None, None, None], alpha1, dir1)
    answer = combo(answer, alpha2, dir2)
    answer = combo(answer, alpha3, dir3)
    return answer, gamma3


def body(stiffness, mass_matrix, omega_table, assignment, adjoint_load, forward_state, owner_index):
    n_freq = lax.axis_size("freq")
    n_sub = lax.axis_size("sx") * lax.axis_size("sy")
    slots, faces, face_len = adjoint_load.shape[2], adjoint_load.shape[4], adjoint_load.shape[5]
    order = faces * face_len
    run = face_len // n_freq
    width = faces * run
    count = n_freq * slots * 2
    own = 2 * slots
    me = lax.axis_index("freq")

    load = jnp.swapaxes(adjoint_load[0, 0].astype(BF), 0, 1).reshape(own, faces, n_freq, run)
    load = jnp.swapaxes(load, 1, 2).reshape(own, order)
    tags = jnp.broadcast_to(assignment.astype(BF)[None, :], (2, slots)).reshape(own, 1)
    packet = jnp.concatenate([load, jnp.broadcast_to(tags, (own, 128))], axis=1)
    field = exchange(jnp.broadcast_to(packet[None], (n_freq, *packet.shape)), "freq")
    pair = arrange(stiffness[0, 0], mass_matrix[0, 0], faces, n_freq)
    slot_tags = field[:, :, order].reshape(count).astype(jnp.int32)
    matches = slot_tags[:, None] == jnp.arange(omega_table.shape[0], dtype=jnp.int32)[None, :]
    omega_rows = jnp.sum(jnp.where(matches, omega_table[None, :], 0.0), axis=1, keepdims=True)

    def inside(axis, at):
        return jnp.where(lax.axis_index(axis) == at, 1.0, 0.5).astype(F32)

    face_weight = jnp.stack(
        [
            inside("sx", 0),
            inside("sx", lax.axis_size("sx") - 1),
            inside("sy", 0),
            inside("sy", lax.axis_size("sy") - 1),
        ]
    )
    weight = jnp.repeat(face_weight, run)[None, :]
    once = jnp.where(face_weight < 1.0, jnp.array([1.0, 0.0, 1.0, 0.0], F32), 1.0)
    weight_once = jnp.repeat(once, run)[None, :]

    def local_of(field, sign, by_slot=False, once=False):
        local, *face_vals = apply_local(field, pair, omega_rows, sign, faces, by_slot)
        return local, swap_faces(face_vals, once)

    def part_sum(rows):
        return jnp.sum(rows.reshape(-1, 2, slots, rows.shape[-1]), axis=1)

    def to_rows(values):
        wide = jnp.broadcast_to(values[:, None], (n_freq, 2, slots, values.shape[-1]))
        return wide.reshape(count, values.shape[-1])

    local, halo = local_of(field, -1.0, by_slot=True)
    u0, send = finish(local, halo, n_freq, send=F32)
    sent0 = exchange(send, "freq")
    local, halo = local_of(sent0, 1.0)
    w0, send = finish(local, halo, n_freq, send=F32)
    local, halo = local_of(exchange(send, "freq"), -1.0)
    u1, send = finish(local, halo, n_freq, send=F32)
    sent1 = exchange(send, "freq")
    local, halo = local_of(sent1, 1.0)
    products = ((0, 0), (0, 1), (1, 1), (2, 2), (2, 3), (3, 3))
    w1, send = finish(
        local, halo, n_freq, earlier=(u0, u1, w0), products=products, weight=weight, send=F32
    )
    sent = exchange(send, "freq")
    sums = jnp.sum(sent[:, :, width : width + len(products)], axis=0)
    sums = part_sum(sums)
    sums = total(total(sums.reshape(-1), "sy"), "sx").reshape(n_freq, slots, len(products))
    g = {(0, 0): sums[..., 0], (0, 1): sums[..., 1], (1, 1): sums[..., 2]}
    w = {(0, 0): sums[..., 3], (0, 1): sums[..., 4], (1, 1): sums[..., 5]}
    alpha0, _, _, beta0, _, alpha1 = first_scalars(g, w)
    coefs = to_rows(
        jnp.stack(
            [jnp.ones_like(alpha0), -(alpha0 + alpha1 * (1.0 + beta0)), alpha0 * alpha1], axis=-1
        )
    )
    local, halo = local_of(sent, -1.0)
    u2, send = finish(local, halo, n_freq, earlier=(u0, u1), combine=(0, 1), coefs=coefs)
    sent2 = exchange(send, "freq")
    local, halo = local_of(sent2, 1.0)
    w2, send = finish(local, halo, n_freq)
    local, halo = local_of(exchange(send, "freq"), -1.0)
    u3, send = finish(local, halo, n_freq)
    sent3 = exchange(send, "freq")
    local, halo = local_of(sent3, 1.0, once=True)
    later = ((0, 2), (1, 2), (2, 2), (0, 3), (1, 3), (2, 3), (3, 3))
    products = later + tuple((4 + i, 4 + j) for i, j in later)
    (rows,) = finish(
        local, halo, n_freq, earlier=(u0, u1, u2, u3, w0, w1, w2), products=products,
        weight=weight_once, keep=False, send=None,
    )
    rows = part_sum(rows[:, : len(products)]).reshape(n_freq, slots * len(products))
    ours = jnp.sum(exchange(rows, "freq"), axis=0)
    ours = total(total(ours, "sy"), "sx").reshape(slots, len(products))
    mine = lax.dynamic_index_in_dim(sums, me, 0, keepdims=False)
    g = {(0, 0): mine[:, 0], (0, 1): mine[:, 1], (1, 1): mine[:, 2]}
    w = {(0, 0): mine[:, 3], (0, 1): mine[:, 4], (1, 1): mine[:, 5]}
    for at, key in enumerate(later):
        g[key] = ours[:, at]
        w[key] = ours[:, len(later) + at]
    answer, gamma = last_scalars(g, w)
    residual_level = jnp.log(gamma / float(n_sub * 2 * order))

    adjoint = 0.0
    for values, sent in zip(answer, (sent0, sent1, sent2, sent3)):
        block = lax.dynamic_slice_in_dim(sent, me * own, own, axis=1)[:, :, :width].astype(F32)
        adjoint = adjoint + block * jnp.tile(values, 2)[None, :, None]
    adjoint = adjoint.reshape(n_freq, 2, slots, faces, run)
    adjoint = jnp.transpose(adjoint, (2, 1, 3, 0, 4)).reshape(slots, 2, faces, face_len)

    state = forward_state[0, 0].astype(F32)
    adj_real, adj_imag = adjoint[:, 0], adjoint[:, 1]
    state_real, state_imag = state[:, 0], state[:, 1]
    term = (
        adj_real * state_real
        - adj_imag * state_imag
        - LOSS_FACTOR * (adj_real * state_imag + adj_imag * state_real)
    )
    dof_total = jnp.sum(term, axis=0).reshape(1, order)
    owner = owner_index[0, 0].reshape(1, order)
    high = jnp.arange(DE_SUB // LOW, dtype=jnp.int32)[:, None]
    low = jnp.arange(LOW, dtype=jnp.int32)[:, None]
    spread = jnp.where(lax.div(owner, LOW) == high, dof_total, 0.0)
    places = jnp.where(lax.rem(owner, LOW) == low, 1.0, 0.0)
    partial_grad = lax.dot_general(
        spread, places, (((1,), (1,)), ((), ())), precision=lax.Precision.HIGHEST
    )
    grad_factor = (DE_SUB / (slots * n_freq * order)) ** 0.5
    partial_grad = (-grad_factor * partial_grad).reshape(n_freq, DE_SUB // n_freq)
    gradient = jnp.sum(exchange(partial_grad, "freq"), axis=0)
    return (adjoint[None, None], gradient[None, None], residual_level)


def solution(mesh):
    return jax.shard_map(
        body,
        mesh=mesh,
        in_specs=(
            P("sx", "sy", None, "freq"),
            P("sx", "sy", None, "freq"),
            P(),
            P("freq"),
            P("sx", "sy", "freq", None, None, None),
            P("sx", "sy", "freq", None, None, None),
            P("sx", "sy", None, None),
        ),
        out_specs=(P("sx", "sy", "freq", None, None, None), P("sx", "sy", "freq"), P("freq")),
        check_vma=False,
    )
```

```python
import functools

import jax
import jax.numpy as jnp
from jax import lax
from jax.experimental import pallas as pl
from jax.experimental.pallas import tpu as pltpu
from jax.sharding import PartitionSpec as P

DE_SUB = 1728
LOSS_FACTOR = 0.3
LOW = 64
BF = jnp.bfloat16
F32 = jnp.float32


def params():
    return pltpu.CompilerParams(vmem_limit_bytes=24 * 1024 * 1024)


def arrange_kernel(stiff_ref, mass_ref, out_ref, order_ref):
    faces, _, run, width = stiff_ref.shape

    @pl.when(pl.program_id(0) == 0)
    def _():
        source = lax.broadcasted_iota(jnp.int32, (width, width), 0)
        target = lax.broadcasted_iota(jnp.int32, (width, width), 1)
        wanted = faces * lax.rem(target, run) + lax.div(target, run)
        order_ref[...] = jnp.where(source == wanted, 1.0, 0.0).astype(BF)

    for at, ref in enumerate((stiff_ref, mass_ref)):
        rows = ref[...].reshape(faces * run, width)
        moved = jnp.dot(rows, order_ref[...], preferred_element_type=F32)
        out_ref[0, :, at * width : (at + 1) * width] = moved.astype(BF)


def arrange(stiffness, mass_matrix, faces, n_freq):
    order, width = stiffness.shape
    run = order // (faces * n_freq)
    block = pl.BlockSpec((faces, 1, run, width), lambda d: (0, d, 0, 0))
    return pl.pallas_call(
        arrange_kernel,
        grid=(n_freq,),
        in_specs=[block, block],
        out_specs=pl.BlockSpec((1, width, 2 * width), lambda d: (d, 0, 0)),
        out_shape=jax.ShapeDtypeStruct((n_freq, width, 2 * width), BF),
        scratch_shapes=[pltpu.VMEM((width, width), BF)],
        compiler_params=params(),
        name="arrange",
    )(
        stiffness.reshape(faces, n_freq, run, width),
        mass_matrix.reshape(faces, n_freq, run, width),
    )


def apply_kernel(sign, faces, by_slot, sides, *refs):
    field_ref, pair_ref, omega_ref, odd_ref, local_ref = refs[:5]
    face_refs = refs[5:-2]
    held_ref, sems = refs[-2:]
    n_freq = pair_ref.shape[0]
    count, width = local_ref.shape
    copies = [
        pltpu.make_async_copy(pair_ref.at[d], held_ref.at[d], sems.at[d]) for d in range(n_freq)
    ]
    for copy in copies:
        copy.start()
    total_sum = None
    for d in range(n_freq):
        if by_slot:
            rows = field_ref[:, :, d * width : (d + 1) * width].reshape(count, width)
        else:
            rows = field_ref[d, :count, :]
        copies[d].wait()
        product = jnp.dot(rows, held_ref[d], preferred_element_type=F32)
        total_sum = product if total_sum is None else total_sum + product
    stiff_part = total_sum[:, :width]
    mass_part = total_sum[:, width:]
    row = lax.broadcasted_iota(jnp.int32, (count, width), 0)
    real = lax.rem(row, 8) < 4
    other = jnp.where(
        real, -pltpu.roll(stiff_part, count - 4, 0), pltpu.roll(stiff_part, 4, 0)
    )
    local = stiff_part + (sign * LOSS_FACTOR) * other - omega_ref[...] * mass_part
    local_ref[...] = local
    run = width // faces
    west, east, south, north = (local[:, f * run : (f + 1) * run] for f in range(faces))
    if sides:
        face_refs[0][...] = east
        face_refs[1][...] = north
        return
    odd_x, odd_y = odd_ref[0] == 1, odd_ref[1] == 1
    face_refs[0][...] = jnp.where(odd_x, west, east)
    face_refs[1][...] = jnp.where(odd_x, east, west)
    face_refs[2][...] = jnp.where(odd_y, south, north)
    face_refs[3][...] = jnp.where(odd_y, north, south)


def apply_local(field, pair, omega_rows, odd, sign, faces, by_slot=False, sides=False):
    n_freq, width, double = pair.shape
    count = omega_rows.shape[0]
    run = width // faces
    n_out = 2 if sides else faces
    vmem = pl.BlockSpec(memory_space=pltpu.VMEM)
    return pl.pallas_call(
        functools.partial(apply_kernel, sign, faces, by_slot, sides),
        in_specs=[
            vmem,
            pl.BlockSpec(memory_space=pltpu.HBM),
            vmem,
            pl.BlockSpec(memory_space=pltpu.SMEM),
        ],
        out_specs=[vmem] * (1 + n_out),
        out_shape=[jax.ShapeDtypeStruct((count, width), F32)]
        + [jax.ShapeDtypeStruct((count, run), F32)] * n_out,
        scratch_shapes=[
            pltpu.VMEM((n_freq, width, double), BF),
            pltpu.SemaphoreType.DMA((n_freq,)),
        ],
        compiler_params=params(),
        name="apply_local",
    )(field, pair, omega_rows, odd)


def permute(values, axis, pairs):
    return lax.ppermute(values, axis, pairs) if pairs else jnp.zeros_like(values)


def swap_faces(face_vals):
    out = []
    for axis, (near, far) in (("sx", face_vals[:2]), ("sy", face_vals[2:])):
        count = lax.axis_size(axis)
        low = [(i, i ^ 1) for i in range(count)]
        high = [(i, ((i + 1) ^ 1) - 1) for i in range(1, count - 1)]
        out += [permute(near, axis, low), permute(far, axis, high)]
    return out


def pass_faces(face_vals):
    out = []
    for axis, values in zip(("sx", "sy"), face_vals):
        pairs = [(i, i + 1) for i in range(lax.axis_size(axis) - 1)]
        out.append(permute(values, axis, pairs))
    return out


def finish_kernel(plan, faces, n_in, copies, *refs):
    combine, products, keep, send, n_halo = plan
    odd_ref, local_ref = refs[:2]
    halo = [ref[...] for ref in refs[2 : 2 + n_halo]]
    at = 2 + n_halo
    earlier = refs[at : at + n_in]
    at += n_in
    coefs_ref = weight_ref = None
    if combine:
        coefs_ref, at = refs[at], at + 1
    if products:
        weight_ref, at = refs[at], at + 1
    outs = list(refs[at:])
    if n_halo == faces:
        odd_x, odd_y = odd_ref[0] == 1, odd_ref[1] == 1
        near_x, far_x, near_y, far_y = halo
        halo = [
            jnp.where(odd_x, near_x, far_x),
            jnp.where(odd_x, far_x, near_x),
            jnp.where(odd_y, near_y, far_y),
            jnp.where(odd_y, far_y, near_y),
        ]
    else:
        none = jnp.zeros_like(halo[0])
        halo = [halo[0], none, halo[1], none]
    vector = local_ref[...] + jnp.concatenate(halo, axis=1)
    count, width = vector.shape
    known = [ref[...] for ref in earlier]
    if combine:
        vector = vector * coefs_ref[:, len(combine) : len(combine) + 1]
        for slot, which in enumerate(combine):
            vector = vector + known[which] * coefs_ref[:, slot : slot + 1]
    known.append(vector)
    if keep:
        outs.pop(0)[...] = vector
    sums = None
    if products:
        weight = jnp.broadcast_to(weight_ref[...], (8, width))
        high = -(-len(products) // 8) * 8
        place = lax.broadcasted_iota(jnp.int32, (high, count), 0)
        sums = jnp.zeros((high, count), F32)
        for slot, (left, right) in enumerate(products):
            value = lax.dot_general(
                weight,
                known[left] * known[right],
                (((1,), (1,)), ((), ())),
                precision=lax.Precision.HIGHEST,
                preferred_element_type=F32,
            )
            sums = jnp.where(place == slot, value[:1], sums)
    if send:
        sent = vector.astype(BF)
        out = outs.pop(0)
        extra = None
        if products:
            parts = []
            for _ in range(3):
                part = sums.astype(BF)
                parts.append(part.astype(F32))
                sums = sums - parts[-1]
            parts.append(jnp.zeros((sums.shape[0], width - 3 * count), F32))
            extra = jnp.concatenate(parts, axis=1).astype(BF)
        for copy in range(copies):
            out[copy, :count, :] = sent
            if extra is not None:
                out[copy, count:, :] = extra
    elif products:
        outs.pop(0)[...] = sums


def finish(
    local, halos, odd, n_freq, faces, earlier=(), combine=(), coefs=None, products=(),
    weight=None, keep=True, send=True,
):
    count, width = local.shape
    args = [odd, local, *halos, *earlier]
    if combine:
        args.append(coefs)
    if products:
        args.append(weight)
    shapes = []
    high = -(-len(products) // 8) * 8
    if keep:
        shapes.append(jax.ShapeDtypeStruct((count, width), F32))
    if send:
        shapes.append(jax.ShapeDtypeStruct((n_freq, count + high, width), BF))
    elif products:
        shapes.append(jax.ShapeDtypeStruct((high, count), F32))
    plan = (tuple(combine), tuple(products), keep, send, len(halos))
    vmem = pl.BlockSpec(memory_space=pltpu.VMEM)
    return pl.pallas_call(
        functools.partial(finish_kernel, plan, faces, len(earlier), n_freq),
        in_specs=[pl.BlockSpec(memory_space=pltpu.SMEM)] + [vmem] * (len(args) - 1),
        out_specs=[vmem] * len(shapes),
        out_shape=shapes,
        compiler_params=params(),
        name="finish",
    )(*args)


def exchange(blocks, axis):
    return lax.all_to_all(blocks, axis, 0, 0, tiled=False)


def total(values, axis):
    count = lax.axis_size(axis)
    return jnp.sum(exchange(jnp.broadcast_to(values[None], (count, *values.shape)), axis), axis=0)


def quad(entries, coefs):
    result = 0.0
    for i, left in enumerate(coefs):
        for j in range(i, len(coefs)):
            if left is None or coefs[j] is None:
                continue
            term = left * coefs[j] * entries[(i, j)]
            result = result + (term if i == j else 2.0 * term)
    return result


def combo(first, scale, second):
    out = []
    for a, b in zip(first, second):
        b = None if b is None else scale * b
        out.append(b if a is None else a if b is None else a + b)
    return out


def unit(at, one):
    return [one if i == at else None for i in range(4)]


def last_scalars(alpha0, beta0, alpha1, g, w):
    one = jnp.ones_like(alpha0)
    res0, res1, res2, lead = (unit(i, one) for i in range(4))
    dir1 = combo(res1, beta0, res0)
    gamma2 = g[(2, 2)]
    beta1 = gamma2 / g[(1, 1)]
    dir2 = combo(res2, beta1, dir1)
    alpha2 = gamma2 / quad(w, dir2)
    image = combo(lead, beta1 / alpha1, combo(res1, -1.0, res2))
    res3 = combo(res2, -alpha2, image)
    gamma3 = quad(g, res3)
    dir3 = combo(res3, gamma3 / gamma2, dir2)
    alpha3 = gamma3 / quad(w, dir3)
    answer = combo([alpha0, None, None, None], alpha1, dir1)
    answer = combo(answer, alpha2, dir2)
    answer = combo(answer, alpha3, dir3)
    return answer, gamma3


def body(stiffness, mass_matrix, omega_table, assignment, adjoint_load, forward_state, owner_index):
    n_freq = lax.axis_size("freq")
    n_sub = lax.axis_size("sx") * lax.axis_size("sy")
    slots, faces, face_len = adjoint_load.shape[2], adjoint_load.shape[4], adjoint_load.shape[5]
    order = faces * face_len
    run = face_len // n_freq
    width = faces * run
    count = n_freq * slots * 2
    own = 2 * slots
    me = lax.axis_index("freq")

    load = jnp.swapaxes(adjoint_load[0, 0].astype(BF), 0, 1).reshape(own, faces, n_freq, run)
    load = jnp.swapaxes(load, 1, 2).reshape(own, order)
    tags = jnp.broadcast_to(assignment.astype(BF)[None, :], (2, slots)).reshape(own, 1)
    packet = jnp.concatenate([load, jnp.broadcast_to(tags, (own, 128))], axis=1)
    field = exchange(jnp.broadcast_to(packet[None], (n_freq, *packet.shape)), "freq")
    pair = arrange(stiffness[0, 0], mass_matrix[0, 0], faces, n_freq)
    slot_tags = field[:, :, order].reshape(count).astype(jnp.int32)
    matches = slot_tags[:, None] == jnp.arange(omega_table.shape[0], dtype=jnp.int32)[None, :]
    omega_rows = jnp.sum(jnp.where(matches, omega_table[None, :], 0.0), axis=1, keepdims=True)

    def inside(axis, at):
        return jnp.where(lax.axis_index(axis) == at, 1.0, 0.5).astype(F32)

    face_weight = jnp.stack(
        [
            inside("sx", 0),
            inside("sx", lax.axis_size("sx") - 1),
            inside("sy", 0),
            inside("sy", lax.axis_size("sy") - 1),
        ]
    )
    weight = jnp.repeat(face_weight, run)[None, :]
    once = jnp.where(face_weight < 1.0, jnp.array([1.0, 0.0, 1.0, 0.0], F32), 1.0)
    weight_once = jnp.repeat(once, run)[None, :]

    odd = jnp.stack([lax.rem(lax.axis_index(axis), 2) for axis in ("sx", "sy")]).astype(jnp.int32)

    def step(field, sign, by_slot=False, **how):
        local, *face_vals = apply_local(field, pair, omega_rows, odd, sign, faces, by_slot)
        return finish(local, swap_faces(face_vals), odd, n_freq, faces, **how)

    def by_slots(sums, n_products):
        return jnp.sum(sums[:n_products].reshape(n_products, n_freq, 2, slots), axis=2)

    def spread(sent, n_products):
        sums = sum(
            jnp.sum(sent[:, count:, k * count : (k + 1) * count].astype(F32), axis=0)
            for k in range(3)
        )
        sums = by_slots(sums, n_products)
        flat = total(total(sums.reshape(-1), "sy"), "sx")
        return flat.reshape(n_products, n_freq, slots)

    def to_rows(values):
        wide = jnp.stack(values, axis=-1)[:, None]
        return jnp.broadcast_to(wide, (n_freq, 2, slots, len(values))).reshape(count, len(values))

    u0, send = step(field, -1.0, by_slot=True)
    sent0 = exchange(send, "freq")
    w0, send = step(sent0, 1.0, earlier=(u0,), products=((0, 0), (1, 1)), weight=weight)
    sent = exchange(send, "freq")
    gamma0, delta0 = spread(sent, 2)
    alpha0 = gamma0 / delta0
    coefs = to_rows([jnp.ones_like(alpha0), -alpha0])
    u1, send = step(sent, -1.0, earlier=(u0,), combine=(0,), coefs=coefs)
    sent1 = exchange(send, "freq")
    w1, send = step(
        sent1, 1.0, earlier=(u1, w0), products=((0, 0), (1, 2), (2, 2)), weight=weight
    )
    sent = exchange(send, "freq")
    gamma1, cross, image1 = spread(sent, 3)
    beta0 = gamma1 / gamma0
    alpha1 = gamma1 / (image1 + beta0 * (2.0 * cross + beta0 * delta0))
    ratio = alpha1 * beta0 / alpha0
    coefs = to_rows([-ratio, 1.0 + ratio, -alpha1])
    u2, send = step(sent, -1.0, earlier=(u0, u1), combine=(0, 1), coefs=coefs)
    sent2 = exchange(send, "freq")
    w2, send = step(sent2, 1.0)
    u3, send = step(exchange(send, "freq"), -1.0)
    sent3 = exchange(send, "freq")
    local, *face_vals = apply_local(sent3, pair, omega_rows, odd, 1.0, faces, sides=True)
    later_g = ((1, 2), (2, 2), (1, 3), (2, 3), (3, 3))
    later_w = ((0, 2), (1, 2), (2, 2), (0, 3), (1, 3), (2, 3), (3, 3))
    products = tuple((i - 1, j - 1) for i, j in later_g) + tuple((3 + i, 3 + j) for i, j in later_w)
    (sums,) = finish(
        local, pass_faces(face_vals), odd, n_freq, faces, earlier=(u1, u2, u3, w0, w1, w2),
        products=products, weight=weight_once, keep=False, send=False,
    )
    sums = by_slots(sums, len(products))
    sums = jnp.swapaxes(sums, 0, 1).reshape(n_freq, len(products) * slots)
    ours = jnp.sum(exchange(sums, "freq"), axis=0)
    ours = total(total(ours, "sy"), "sx").reshape(len(products), slots)
    earlier = jnp.stack([alpha0, beta0, alpha1, gamma1, delta0, cross, image1])
    mine = lax.dynamic_index_in_dim(earlier, me, 1, keepdims=False)
    g = {(1, 1): mine[3]}
    w = {(0, 0): mine[4], (0, 1): mine[5], (1, 1): mine[6]}
    for at, key in enumerate(later_g):
        g[key] = ours[at]
    for at, key in enumerate(later_w):
        w[key] = ours[len(later_g) + at]
    answer, gamma = last_scalars(mine[0], mine[1], mine[2], g, w)
    residual_level = jnp.log(gamma / float(n_sub * 2 * order))

    adjoint = 0.0
    for values, sent in zip(answer, (sent0, sent1, sent2, sent3)):
        block = lax.dynamic_slice_in_dim(sent, me * own, own, axis=1)[:, :, :width].astype(F32)
        adjoint = adjoint + block * jnp.tile(values, 2)[None, :, None]
    adjoint = adjoint.reshape(n_freq, 2, slots, faces, run)
    adjoint = jnp.transpose(adjoint, (2, 1, 3, 0, 4)).reshape(slots, 2, faces, face_len)

    state = forward_state[0, 0].astype(F32)
    adj_real, adj_imag = adjoint[:, 0], adjoint[:, 1]
    state_real, state_imag = state[:, 0], state[:, 1]
    term = (
        adj_real * state_real
        - adj_imag * state_imag
        - LOSS_FACTOR * (adj_real * state_imag + adj_imag * state_real)
    )
    dof_total = jnp.sum(term, axis=0).reshape(1, order)
    owner = owner_index[0, 0].reshape(1, order)
    high = jnp.arange(DE_SUB // LOW, dtype=jnp.int32)[:, None]
    low = jnp.arange(LOW, dtype=jnp.int32)[:, None]
    spread = jnp.where(lax.div(owner, LOW) == high, dof_total, 0.0)
    places = jnp.where(lax.rem(owner, LOW) == low, 1.0, 0.0)
    partial_grad = lax.dot_general(
        spread, places, (((1,), (1,)), ((), ())), precision=lax.Precision.HIGHEST
    )
    grad_factor = (DE_SUB / (slots * n_freq * order)) ** 0.5
    partial_grad = (-grad_factor * partial_grad).reshape(n_freq, DE_SUB // n_freq)
    gradient = jnp.sum(exchange(partial_grad, "freq"), axis=0)
    return (adjoint[None, None], gradient[None, None], residual_level)


def solution(mesh):
    return jax.shard_map(
        body,
        mesh=mesh,
        in_specs=(
            P("sx", "sy", None, "freq"),
            P("sx", "sy", None, "freq"),
            P(),
            P("freq"),
            P("sx", "sy", "freq", None, None, None),
            P("sx", "sy", "freq", None, None, None),
            P("sx", "sy", None, None),
        ),
        out_specs=(P("sx", "sy", "freq", None, None, None), P("sx", "sy", "freq"), P("freq")),
        check_vma=False,
    )
```

```python
import functools

import jax
import jax.numpy as jnp
from jax import lax
from jax.experimental import pallas as pl
from jax.experimental.pallas import tpu as pltpu
from jax.sharding import PartitionSpec as P

DE_SUB = 1728
LOSS_FACTOR = 0.3
LOW = 64
BF = jnp.bfloat16
F32 = jnp.float32


def params():
    return pltpu.CompilerParams(vmem_limit_bytes=24 * 1024 * 1024)


def arrange_kernel(stiff_ref, mass_ref, out_ref, order_ref):
    faces, _, run, width = stiff_ref.shape

    @pl.when(pl.program_id(0) == 0)
    def _():
        source = lax.broadcasted_iota(jnp.int32, (width, width), 0)
        target = lax.broadcasted_iota(jnp.int32, (width, width), 1)
        wanted = faces * lax.rem(target, run) + lax.div(target, run)
        order_ref[...] = jnp.where(source == wanted, 1.0, 0.0).astype(BF)

    for at, ref in enumerate((stiff_ref, mass_ref)):
        rows = ref[...].reshape(faces * run, width)
        moved = jnp.dot(rows, order_ref[...], preferred_element_type=F32)
        out_ref[0, :, at * width : (at + 1) * width] = moved.astype(BF)


def arrange(stiffness, mass_matrix, faces, n_freq):
    order, width = stiffness.shape
    run = order // (faces * n_freq)
    block = pl.BlockSpec((faces, 1, run, width), lambda d: (0, d, 0, 0))
    return pl.pallas_call(
        arrange_kernel,
        grid=(n_freq,),
        in_specs=[block, block],
        out_specs=pl.BlockSpec((1, width, 2 * width), lambda d: (d, 0, 0)),
        out_shape=jax.ShapeDtypeStruct((n_freq, width, 2 * width), BF),
        scratch_shapes=[pltpu.VMEM((width, width), BF)],
        compiler_params=params(),
        name="arrange",
    )(
        stiffness.reshape(faces, n_freq, run, width),
        mass_matrix.reshape(faces, n_freq, run, width),
    )


def odd_masks(odd_ref, shape):
    return [jnp.broadcast_to(odd_ref[i : i + 1, : shape[1]], shape) > 0.5 for i in range(2)]


def apply_kernel(sign, faces, by_slot, sides, *refs):
    field_ref, pair_ref, omega_ref, odd_ref, local_ref = refs[:5]
    face_refs = refs[5:-2]
    held_ref, sems = refs[-2:]
    n_freq = pair_ref.shape[0]
    count, width = local_ref.shape
    copies = [
        pltpu.make_async_copy(pair_ref.at[d], held_ref.at[d], sems.at[d]) for d in range(n_freq)
    ]
    for copy in copies:
        copy.start()
    total_sum = None
    for d in range(n_freq):
        if by_slot:
            rows = field_ref[:, :, d * width : (d + 1) * width].reshape(count, width)
        else:
            rows = field_ref[d, :count, :]
        copies[d].wait()
        product = jnp.dot(rows, held_ref[d], preferred_element_type=F32)
        total_sum = product if total_sum is None else total_sum + product
    stiff_part = total_sum[:, :width]
    mass_part = total_sum[:, width:]
    row = lax.broadcasted_iota(jnp.int32, (count, width), 0)
    real = lax.rem(row, 8) < 4
    other = jnp.where(
        real, -pltpu.roll(stiff_part, count - 4, 0), pltpu.roll(stiff_part, 4, 0)
    )
    local = stiff_part + (sign * LOSS_FACTOR) * other - omega_ref[...] * mass_part
    local_ref[...] = local
    run = width // faces
    west, east, south, north = (local[:, f * run : (f + 1) * run] for f in range(faces))
    if sides:
        face_refs[0][...] = east
        face_refs[1][...] = north
        return
    odd_x, odd_y = odd_masks(odd_ref, west.shape)
    face_refs[0][...] = jnp.where(odd_x, west, east)
    face_refs[1][...] = jnp.where(odd_x, east, west)
    face_refs[2][...] = jnp.where(odd_y, south, north)
    face_refs[3][...] = jnp.where(odd_y, north, south)


def apply_local(field, pair, omega_rows, odd, sign, faces, by_slot=False, sides=False):
    n_freq, width, double = pair.shape
    count = omega_rows.shape[0]
    run = width // faces
    n_out = 2 if sides else faces
    vmem = pl.BlockSpec(memory_space=pltpu.VMEM)
    return pl.pallas_call(
        functools.partial(apply_kernel, sign, faces, by_slot, sides),
        in_specs=[
            vmem,
            pl.BlockSpec(memory_space=pltpu.HBM),
            vmem,
            vmem,
        ],
        out_specs=[vmem] * (1 + n_out),
        out_shape=[jax.ShapeDtypeStruct((count, width), F32)]
        + [jax.ShapeDtypeStruct((count, run), F32)] * n_out,
        scratch_shapes=[
            pltpu.VMEM((n_freq, width, double), BF),
            pltpu.SemaphoreType.DMA((n_freq,)),
        ],
        compiler_params=params(),
        name="apply_local",
    )(field, pair, omega_rows, odd)


def permute(values, axis, pairs):
    return lax.ppermute(values, axis, pairs) if pairs else jnp.zeros_like(values)


def swap_faces(face_vals):
    out = []
    for axis, (near, far) in (("sx", face_vals[:2]), ("sy", face_vals[2:])):
        count = lax.axis_size(axis)
        low = [(i, i ^ 1) for i in range(count)]
        high = [(i, ((i + 1) ^ 1) - 1) for i in range(1, count - 1)]
        out += [permute(near, axis, low), permute(far, axis, high)]
    return out


def pass_faces(face_vals):
    out = []
    for axis, values in zip(("sx", "sy"), face_vals):
        pairs = [(i, i + 1) for i in range(lax.axis_size(axis) - 1)]
        out.append(permute(values, axis, pairs))
    return out


def finish_kernel(plan, faces, n_in, copies, *refs):
    combine, products, keep, send, n_halo = plan
    odd_ref, local_ref = refs[:2]
    halo = [ref[...] for ref in refs[2 : 2 + n_halo]]
    at = 2 + n_halo
    earlier = refs[at : at + n_in]
    at += n_in
    coefs_ref = weight_ref = None
    if combine:
        coefs_ref, at = refs[at], at + 1
    if products:
        weight_ref, at = refs[at], at + 1
    outs = list(refs[at:])
    if n_halo == faces:
        near_x, far_x, near_y, far_y = halo
        odd_x, odd_y = odd_masks(odd_ref, near_x.shape)
        halo = [
            jnp.where(odd_x, near_x, far_x),
            jnp.where(odd_x, far_x, near_x),
            jnp.where(odd_y, near_y, far_y),
            jnp.where(odd_y, far_y, near_y),
        ]
    else:
        none = jnp.zeros_like(halo[0])
        halo = [halo[0], none, halo[1], none]
    vector = local_ref[...] + jnp.concatenate(halo, axis=1)
    count, width = vector.shape
    known = [ref[...] for ref in earlier]
    if combine:
        vector = known[0] - coefs_ref[...] * vector
    known.append(vector)
    if keep:
        outs.pop(0)[...] = vector
    sums = None
    if products:
        weighted = {left: known[left] * weight_ref[...] for left, _ in products}
        ones = jnp.ones((8, 128), F32)
        high = -(-len(products) // 8) * 8
        place = lax.broadcasted_iota(jnp.int32, (high, count), 0)
        sums = jnp.zeros((high, count), F32)
        for slot, (left, right) in enumerate(products):
            value = weighted[left] * known[right]
            value = sum(value[:, k : k + 128] for k in range(0, width, 128))
            value = lax.dot_general(
                ones,
                value,
                (((1,), (1,)), ((), ())),
                precision=lax.Precision.HIGHEST,
                preferred_element_type=F32,
            )
            sums = jnp.where(place == slot, value[:1], sums)
    if send:
        sent = vector.astype(BF)
        out = outs.pop(0)
        extra = None
        if products:
            parts = []
            for _ in range(3):
                part = sums.astype(BF)
                parts.append(part.astype(F32))
                sums = sums - parts[-1]
            parts.append(jnp.zeros((sums.shape[0], width - 3 * count), F32))
            extra = jnp.concatenate(parts, axis=1).astype(BF)
        for copy in range(copies):
            out[copy, :count, :] = sent
            if extra is not None:
                out[copy, count:, :] = extra
    elif products:
        outs.pop(0)[...] = sums


def finish(
    local, halos, odd, n_freq, faces, earlier=(), scale=None, products=(),
    weight=None, keep=True, send=True,
):
    count, width = local.shape
    args = [odd, local, *halos, *earlier]
    if scale is not None:
        args.append(scale)
    if products:
        args.append(weight)
    shapes = []
    high = -(-len(products) // 8) * 8
    if keep:
        shapes.append(jax.ShapeDtypeStruct((count, width), F32))
    if send:
        shapes.append(jax.ShapeDtypeStruct((n_freq, count + high, width), BF))
    elif products:
        shapes.append(jax.ShapeDtypeStruct((high, count), F32))
    plan = (scale is not None, tuple(products), keep, send, len(halos))
    vmem = pl.BlockSpec(memory_space=pltpu.VMEM)
    return pl.pallas_call(
        functools.partial(finish_kernel, plan, faces, len(earlier), n_freq),
        in_specs=[vmem] * len(args),
        out_specs=[vmem] * len(shapes),
        out_shape=shapes,
        compiler_params=params(),
        name="finish",
    )(*args)


def exchange(blocks, axis):
    return lax.all_to_all(blocks, axis, 0, 0, tiled=False)


def total(values, axis):
    count = lax.axis_size(axis)
    return jnp.sum(exchange(jnp.broadcast_to(values[None], (count, *values.shape)), axis), axis=0)


def quad(entries, coefs):
    result = 0.0
    for i, left in enumerate(coefs):
        for j in range(i, len(coefs)):
            if left is None or coefs[j] is None:
                continue
            term = left * coefs[j] * entries[(i, j)]
            result = result + (term if i == j else 2.0 * term)
    return result


def combo(first, scale, second):
    out = []
    for a, b in zip(first, second):
        b = None if b is None else scale * b
        out.append(b if a is None else a if b is None else a + b)
    return out


def solve(theta, g, w):
    one = jnp.ones_like(theta)
    residual = direction = [one, None, None, None]
    answer = [None] * 4
    gamma = quad(g, residual)
    for iteration in range(4):
        alpha = gamma / quad(w, direction)
        answer = combo(answer, alpha, direction)
        if iteration < 3:
            below = [None] + direction[:3]
            image = combo([None if c is None else theta * c for c in direction], -theta, below)
            residual = combo(residual, -alpha, image)
            gamma_next = quad(g, residual)
            direction = combo(residual, gamma_next / gamma, direction)
            gamma = gamma_next
    return answer, gamma


def body(stiffness, mass_matrix, omega_table, assignment, adjoint_load, forward_state, owner_index):
    n_freq = lax.axis_size("freq")
    n_sub = lax.axis_size("sx") * lax.axis_size("sy")
    slots, faces, face_len = adjoint_load.shape[2], adjoint_load.shape[4], adjoint_load.shape[5]
    order = faces * face_len
    run = face_len // n_freq
    width = faces * run
    count = n_freq * slots * 2
    own = 2 * slots
    me = lax.axis_index("freq")

    load = jnp.swapaxes(adjoint_load[0, 0].astype(BF), 0, 1).reshape(own, faces, n_freq, run)
    load = jnp.swapaxes(load, 1, 2).reshape(own, order)
    tags = jnp.broadcast_to(assignment.astype(BF)[None, :], (2, slots)).reshape(own, 1)
    packet = jnp.concatenate([load, jnp.broadcast_to(tags, (own, 128))], axis=1)
    field = exchange(jnp.broadcast_to(packet[None], (n_freq, *packet.shape)), "freq")
    pair = arrange(stiffness[0, 0], mass_matrix[0, 0], faces, n_freq)
    pair = pltpu.with_memory_space_constraint(pair, pltpu.HBM)
    slot_tags = field[:, :, order].reshape(count).astype(jnp.int32)
    matches = slot_tags[:, None] == jnp.arange(omega_table.shape[0], dtype=jnp.int32)[None, :]
    omega_rows = jnp.sum(jnp.where(matches, omega_table[None, :], 0.0), axis=1, keepdims=True)

    def inside(axis, at):
        return jnp.where(lax.axis_index(axis) == at, 1.0, 0.5).astype(F32)

    face_weight = jnp.stack(
        [
            inside("sx", 0),
            inside("sx", lax.axis_size("sx") - 1),
            inside("sy", 0),
            inside("sy", lax.axis_size("sy") - 1),
        ]
    )
    weight = jnp.repeat(face_weight, run)[None, :]
    once = jnp.where(face_weight < 1.0, jnp.array([1.0, 0.0, 1.0, 0.0], F32), 1.0)
    weight_once = jnp.repeat(once, run)[None, :]

    odd = jnp.stack([lax.rem(lax.axis_index(axis), 2) for axis in ("sx", "sy")]).astype(F32)
    odd = jnp.broadcast_to(odd[:, None], (2, 128))

    def step(field, sign, by_slot=False, **how):
        local, *face_vals = apply_local(field, pair, omega_rows, odd, sign, faces, by_slot)
        return finish(local, swap_faces(face_vals), odd, n_freq, faces, **how)

    def by_slots(sums, n_products):
        return jnp.sum(sums[:n_products].reshape(n_products, n_freq, 2, slots), axis=2)

    def freq_sums(sent, n_products):
        sums = sum(
            jnp.sum(sent[:, count:, k * count : (k + 1) * count].astype(F32), axis=0)
            for k in range(3)
        )
        return by_slots(sums, n_products)

    def to_rows(values):
        return jnp.broadcast_to(values[:, None], (n_freq, 2, slots)).reshape(count, 1)

    (u0, send) = step(field, -1.0, by_slot=True)
    sent0 = exchange(send, "freq")
    (send,) = step(
        sent0, 1.0, earlier=(u0,), products=((0, 0), (1, 1)), weight=weight, keep=False
    )
    sent = exchange(send, "freq")
    flat = total(total(freq_sums(sent, 2).reshape(-1), "sy"), "sx")
    gamma0, delta0 = flat.reshape(2, n_freq, slots)
    scale = to_rows(gamma0 / delta0)
    u1, send = step(sent, -1.0, earlier=(u0,), scale=scale)
    sent1 = exchange(send, "freq")
    (send,) = step(sent1, 1.0, keep=False)
    u2, send = step(exchange(send, "freq"), -1.0, earlier=(u1,), scale=scale)
    sent2 = exchange(send, "freq")
    (send,) = step(sent2, 1.0, keep=False)
    keys = ((0, 1), (0, 2), (0, 3), (1, 1), (1, 2), (1, 3), (2, 2), (2, 3), (3, 3))
    at = {2: 0, 0: 1, 1: 2, 3: 3}
    (send,) = step(
        exchange(send, "freq"), -1.0, earlier=(u2, u0, u1), scale=scale,
        products=tuple((at[i], at[j]) for i, j in keys), weight=weight, keep=False,
    )
    sent3 = exchange(send, "freq")
    local, *face_vals = apply_local(sent3, pair, omega_rows, odd, 1.0, faces, sides=True)
    (sums,) = finish(
        local, pass_faces(face_vals), odd, n_freq, faces, products=((0, 0),), weight=weight_once,
        keep=False, send=False,
    )
    sums = jnp.sum(exchange(by_slots(sums, 1)[0], "freq"), axis=0)
    others = lax.dynamic_index_in_dim(freq_sums(sent3, len(keys)), me, 1, keepdims=False)
    sums = jnp.concatenate([others, sums[None]], axis=0).reshape(-1)
    sums = total(total(sums, "sy"), "sx").reshape(len(keys) + 1, slots)
    own_gamma = lax.dynamic_index_in_dim(gamma0, me, 0, keepdims=False)
    own_delta = lax.dynamic_index_in_dim(delta0, me, 0, keepdims=False)
    theta = own_delta / own_gamma
    g = {key: sums[k] for k, key in enumerate(keys)}
    g[(0, 0)] = own_gamma
    w = {
        (i, j): theta * (g[(i, j)] - g[(min(i + 1, j), max(i + 1, j))])
        for i in range(3)
        for j in range(i, 4)
    }
    w[(0, 0)] = own_delta
    w[(3, 3)] = sums[len(keys)]
    answer, gamma = solve(theta, g, w)
    residual_level = jnp.log(gamma / float(n_sub * 2 * order))

    adjoint = 0.0
    for values, sent in zip(answer, (sent0, sent1, sent2, sent3)):
        block = lax.dynamic_slice_in_dim(sent, me * own, own, axis=1).astype(F32)
        adjoint = adjoint + block * jnp.tile(values, 2)[None, :, None]
    adjoint = adjoint.reshape(n_freq, 2, slots, faces, run)
    adjoint = jnp.transpose(adjoint, (2, 1, 3, 0, 4)).reshape(slots, 2, faces, face_len)

    state = forward_state[0, 0].astype(F32)
    adj_real, adj_imag = adjoint[:, 0], adjoint[:, 1]
    state_real, state_imag = state[:, 0], state[:, 1]
    term = (
        adj_real * state_real
        - adj_imag * state_imag
        - LOSS_FACTOR * (adj_real * state_imag + adj_imag * state_real)
    )
    dof_total = jnp.sum(term, axis=0).reshape(1, order)
    owner = owner_index[0, 0].reshape(1, order)
    high = jnp.arange(DE_SUB // LOW, dtype=jnp.int32)[:, None]
    low = jnp.arange(LOW, dtype=jnp.int32)[:, None]
    spread = jnp.where(lax.div(owner, LOW) == high, dof_total, 0.0)
    places = jnp.where(lax.rem(owner, LOW) == low, 1.0, 0.0)
    partial_grad = lax.dot_general(
        spread, places, (((1,), (1,)), ((), ())), precision=lax.Precision.HIGHEST
    )
    grad_factor = (DE_SUB / (slots * n_freq * order)) ** 0.5
    partial_grad = (-grad_factor * partial_grad).reshape(n_freq, DE_SUB // n_freq)
    gradient = jnp.sum(exchange(partial_grad, "freq"), axis=0)
    return (adjoint[None, None], gradient[None, None], residual_level)


def solution(mesh):
    return jax.shard_map(
        body,
        mesh=mesh,
        in_specs=(
            P("sx", "sy", None, "freq"),
            P("sx", "sy", None, "freq"),
            P(),
            P("freq"),
            P("sx", "sy", "freq", None, None, None),
            P("sx", "sy", "freq", None, None, None),
            P("sx", "sy", None, None),
        ),
        out_specs=(P("sx", "sy", "freq", None, None, None), P("sx", "sy", "freq"), P("freq")),
        check_vma=False,
    )
```

```python
import functools

import jax
import jax.numpy as jnp
from jax import lax
from jax.experimental import pallas as pl
from jax.experimental.pallas import tpu as pltpu
from jax.sharding import PartitionSpec as P

DE_SUB = 1728
LOSS_FACTOR = 0.3
LOW = 64
BF = jnp.bfloat16
F32 = jnp.float32


def params():
    return pltpu.CompilerParams(vmem_limit_bytes=24 * 1024 * 1024)


def arrange_kernel(stiff_ref, mass_ref, stiff_out, mass_out, order_ref):
    faces, _, run, width = stiff_ref.shape

    @pl.when(pl.program_id(0) == 0)
    def _():
        source = lax.broadcasted_iota(jnp.int32, (width, width), 0)
        target = lax.broadcasted_iota(jnp.int32, (width, width), 1)
        wanted = faces * lax.rem(target, run) + lax.div(target, run)
        order_ref[...] = jnp.where(source == wanted, 1.0, 0.0).astype(BF)

    for ref, out_ref in ((stiff_ref, stiff_out), (mass_ref, mass_out)):
        rows = ref[...].reshape(faces * run, width)
        moved = jnp.dot(rows, order_ref[...], preferred_element_type=F32)
        out_ref[0] = moved.astype(BF)


def arrange(stiffness, mass_matrix, faces, n_freq):
    order, width = stiffness.shape
    run = order // (faces * n_freq)
    block = pl.BlockSpec((faces, 1, run, width), lambda d: (0, d, 0, 0))
    return pl.pallas_call(
        arrange_kernel,
        grid=(n_freq,),
        in_specs=[block, block],
        out_specs=[pl.BlockSpec((1, width, width), lambda d: (d, 0, 0))] * 2,
        out_shape=[jax.ShapeDtypeStruct((n_freq, width, width), BF)] * 2,
        scratch_shapes=[pltpu.VMEM((width, width), BF)],
        compiler_params=params(),
        name="arrange",
    )(
        stiffness.reshape(faces, n_freq, run, width),
        mass_matrix.reshape(faces, n_freq, run, width),
    )


def odd_masks(odd_ref, shape):
    return [jnp.broadcast_to(odd_ref[i : i + 1, : shape[1]], shape) > 0.5 for i in range(2)]


def apply_kernel(sign, faces, by_slot, sides, *refs):
    field_ref, stiff_ref, mass_ref, omega_ref, odd_ref, local_ref = refs[:6]
    face_refs = refs[6:-2]
    held_ref, sems = refs[-2:]
    n_freq = stiff_ref.shape[0]
    count, width = local_ref.shape
    copies = [
        pltpu.make_async_copy(mass_ref.at[d], held_ref.at[d], sems.at[d]) for d in range(n_freq)
    ]
    for copy in copies:
        copy.start()
    def product(matrix_ref, arrive):
        result = None
        for d in range(n_freq):
            if by_slot:
                rows = field_ref[:, :, d * width : (d + 1) * width].reshape(count, width)
            else:
                rows = field_ref[d, :count, :]
            if arrive:
                copies[d].wait()
            part = jnp.dot(rows, matrix_ref[d], preferred_element_type=F32)
            result = part if result is None else result + part
        return result

    stiff_part = product(stiff_ref, False)
    mass_part = product(held_ref, True)
    row = lax.broadcasted_iota(jnp.int32, (count, width), 0)
    real = lax.rem(row, 8) < 4
    other = jnp.where(
        real, -pltpu.roll(stiff_part, count - 4, 0), pltpu.roll(stiff_part, 4, 0)
    )
    local = stiff_part + (sign * LOSS_FACTOR) * other - omega_ref[...] * mass_part
    local_ref[...] = local
    run = width // faces
    west, east, south, north = (local[:, f * run : (f + 1) * run] for f in range(faces))
    if sides:
        face_refs[0][...] = east
        face_refs[1][...] = north
        return
    odd_x, odd_y = odd_masks(odd_ref, west.shape)
    face_refs[0][...] = jnp.where(odd_x, west, east)
    face_refs[1][...] = jnp.where(odd_x, east, west)
    face_refs[2][...] = jnp.where(odd_y, south, north)
    face_refs[3][...] = jnp.where(odd_y, north, south)


def apply_local(field, pair, omega_rows, odd, sign, faces, by_slot=False, sides=False):
    n_freq, width, _ = pair[0].shape
    count = omega_rows.shape[0]
    run = width // faces
    n_out = 2 if sides else faces
    vmem = pl.BlockSpec(memory_space=pltpu.VMEM)
    return pl.pallas_call(
        functools.partial(apply_kernel, sign, faces, by_slot, sides),
        in_specs=[
            vmem,
            vmem,
            pl.BlockSpec(memory_space=pltpu.HBM),
            vmem,
            vmem,
        ],
        out_specs=[vmem] * (1 + n_out),
        out_shape=[jax.ShapeDtypeStruct((count, width), F32)]
        + [jax.ShapeDtypeStruct((count, run), F32)] * n_out,
        scratch_shapes=[
            pltpu.VMEM((n_freq, width, width), BF),
            pltpu.SemaphoreType.DMA((n_freq,)),
        ],
        compiler_params=params(),
        name="apply_local",
    )(field, *pair, omega_rows, odd)


def permute(values, axis, pairs):
    return lax.ppermute(values, axis, pairs) if pairs else jnp.zeros_like(values)


def swap_faces(face_vals):
    out = {}
    for axis, (near, far) in (("sy", face_vals[2:]), ("sx", face_vals[:2])):
        count = lax.axis_size(axis)
        low = [(i, i ^ 1) for i in range(count)]
        high = [(i, ((i + 1) ^ 1) - 1) for i in range(1, count - 1)]
        with jax.named_scope("halo_" + axis):
            out[axis] = [permute(near, axis, low), permute(far, axis, high)]
    return out["sy"] + out["sx"]


def pass_faces(face_vals):
    out = []
    for axis, values in zip(("sx", "sy"), face_vals):
        pairs = [(i, i + 1) for i in range(lax.axis_size(axis) - 1)]
        out.append(permute(values, axis, pairs))
    return out


def finish_kernel(plan, faces, n_in, copies, *refs):
    combine, products, keep, send, n_halo = plan
    odd_ref, local_ref = refs[:2]
    halo = [ref[...] for ref in refs[2 : 2 + n_halo]]
    at = 2 + n_halo
    earlier = refs[at : at + n_in]
    at += n_in
    coefs_ref = weight_ref = None
    if combine:
        coefs_ref, at = refs[at], at + 1
    if products:
        weight_ref, at = refs[at], at + 1
    outs = list(refs[at:])
    if n_halo == faces:
        near_y, far_y, near_x, far_x = halo
        odd_x, odd_y = odd_masks(odd_ref, near_x.shape)
        halo = [
            jnp.where(odd_x, near_x, far_x),
            jnp.where(odd_x, far_x, near_x),
            jnp.where(odd_y, near_y, far_y),
            jnp.where(odd_y, far_y, near_y),
        ]
    else:
        none = jnp.zeros_like(halo[0])
        halo = [halo[0], none, halo[1], none]
    vector = local_ref[...] + jnp.concatenate(halo, axis=1)
    count, width = vector.shape
    known = [ref[...] for ref in earlier]
    if combine:
        vector = known[0] - coefs_ref[...] * vector
    known.append(vector)
    if keep:
        outs.pop(0)[...] = vector
    sums = None
    if products:
        weighted = {left: known[left] * weight_ref[...] for left, _ in products}
        ones = jnp.ones((8, 128), F32)
        high = -(-len(products) // 8) * 8
        place = lax.broadcasted_iota(jnp.int32, (high, count), 0)
        sums = jnp.zeros((high, count), F32)
        for slot, (left, right) in enumerate(products):
            value = weighted[left] * known[right]
            value = sum(value[:, k : k + 128] for k in range(0, width, 128))
            value = lax.dot_general(
                ones,
                value,
                (((1,), (1,)), ((), ())),
                precision=lax.Precision.HIGHEST,
                preferred_element_type=F32,
            )
            sums = jnp.where(place == slot, value[:1], sums)
    if send:
        sent = vector.astype(BF)
        out = outs.pop(0)
        extra = None
        if products:
            parts = []
            for _ in range(3):
                part = sums.astype(BF)
                parts.append(part.astype(F32))
                sums = sums - parts[-1]
            parts.append(jnp.zeros((sums.shape[0], width - 3 * count), F32))
            extra = jnp.concatenate(parts, axis=1).astype(BF)
        for copy in range(copies):
            out[copy, :count, :] = sent
            if extra is not None:
                out[copy, count:, :] = extra
    elif products:
        outs.pop(0)[...] = sums


def finish(
    local, halos, odd, n_freq, faces, earlier=(), scale=None, products=(),
    weight=None, keep=True, send=True,
):
    count, width = local.shape
    args = [odd, local, *halos, *earlier]
    if scale is not None:
        args.append(scale)
    if products:
        args.append(weight)
    shapes = []
    high = -(-len(products) // 8) * 8
    if keep:
        shapes.append(jax.ShapeDtypeStruct((count, width), F32))
    if send:
        shapes.append(jax.ShapeDtypeStruct((n_freq, count + high, width), BF))
    elif products:
        shapes.append(jax.ShapeDtypeStruct((high, count), F32))
    plan = (scale is not None, tuple(products), keep, send, len(halos))
    vmem = pl.BlockSpec(memory_space=pltpu.VMEM)
    return pl.pallas_call(
        functools.partial(finish_kernel, plan, faces, len(earlier), n_freq),
        in_specs=[vmem] * len(args),
        out_specs=[vmem] * len(shapes),
        out_shape=shapes,
        compiler_params=params(),
        name="finish",
    )(*args)


def exchange(blocks, axis):
    return lax.all_to_all(blocks, axis, 0, 0, tiled=False)


def total(values, axis):
    count = lax.axis_size(axis)
    return jnp.sum(exchange(jnp.broadcast_to(values[None], (count, *values.shape)), axis), axis=0)


def quad(entries, coefs):
    result = 0.0
    for i, left in enumerate(coefs):
        for j in range(i, len(coefs)):
            if left is None or coefs[j] is None:
                continue
            term = left * coefs[j] * entries[(i, j)]
            result = result + (term if i == j else 2.0 * term)
    return result


def combo(first, scale, second):
    out = []
    for a, b in zip(first, second):
        b = None if b is None else scale * b
        out.append(b if a is None else a if b is None else a + b)
    return out


def solve(theta, g, w):
    one = jnp.ones_like(theta)
    residual = direction = [one, None, None, None]
    answer = [None] * 4
    gamma = quad(g, residual)
    for iteration in range(4):
        alpha = gamma / quad(w, direction)
        answer = combo(answer, alpha, direction)
        if iteration < 3:
            below = [None] + direction[:3]
            image = combo([None if c is None else theta * c for c in direction], -theta, below)
            residual = combo(residual, -alpha, image)
            gamma_next = quad(g, residual)
            direction = combo(residual, gamma_next / gamma, direction)
            gamma = gamma_next
    return answer, gamma


def body(stiffness, mass_matrix, omega_table, assignment, adjoint_load, forward_state, owner_index):
    n_freq = lax.axis_size("freq")
    n_sub = lax.axis_size("sx") * lax.axis_size("sy")
    slots, faces, face_len = adjoint_load.shape[2], adjoint_load.shape[4], adjoint_load.shape[5]
    order = faces * face_len
    run = face_len // n_freq
    width = faces * run
    count = n_freq * slots * 2
    own = 2 * slots
    me = lax.axis_index("freq")

    load = jnp.swapaxes(adjoint_load[0, 0].astype(BF), 0, 1).reshape(own, faces, n_freq, run)
    load = jnp.swapaxes(load, 1, 2).reshape(own, order)
    tags = jnp.broadcast_to(assignment.astype(BF)[None, :], (2, slots)).reshape(own, 1)
    packet = jnp.concatenate([load, jnp.broadcast_to(tags, (own, 128))], axis=1)
    field = exchange(jnp.broadcast_to(packet[None], (n_freq, *packet.shape)), "freq")
    stiff, mass = arrange(stiffness[0, 0], mass_matrix[0, 0], faces, n_freq)
    pair = (
        pltpu.with_memory_space_constraint(stiff, pltpu.VMEM),
        pltpu.with_memory_space_constraint(mass, pltpu.HBM),
    )
    slot_tags = field[:, :, order].reshape(count).astype(jnp.int32)
    matches = slot_tags[:, None] == jnp.arange(omega_table.shape[0], dtype=jnp.int32)[None, :]
    omega_rows = jnp.sum(jnp.where(matches, omega_table[None, :], 0.0), axis=1, keepdims=True)

    def inside(axis, at):
        return jnp.where(lax.axis_index(axis) == at, 1.0, 0.5).astype(F32)

    face_weight = jnp.stack(
        [
            inside("sx", 0),
            inside("sx", lax.axis_size("sx") - 1),
            inside("sy", 0),
            inside("sy", lax.axis_size("sy") - 1),
        ]
    )
    weight = jnp.repeat(face_weight, run)[None, :]
    once = jnp.where(face_weight < 1.0, jnp.array([1.0, 0.0, 1.0, 0.0], F32), 1.0)
    weight_once = jnp.repeat(once, run)[None, :]

    odd = jnp.stack([lax.rem(lax.axis_index(axis), 2) for axis in ("sx", "sy")]).astype(F32)
    odd = jnp.broadcast_to(odd[:, None], (2, 128))

    def step(field, sign, by_slot=False, **how):
        local, *face_vals = apply_local(field, pair, omega_rows, odd, sign, faces, by_slot)
        return finish(local, swap_faces(face_vals), odd, n_freq, faces, **how)

    def by_slots(sums, n_products):
        return jnp.sum(sums[:n_products].reshape(n_products, n_freq, 2, slots), axis=2)

    def freq_sums(sent, n_products):
        sums = sum(
            jnp.sum(sent[:, count:, k * count : (k + 1) * count].astype(F32), axis=0)
            for k in range(3)
        )
        return by_slots(sums, n_products)

    def to_rows(values):
        return jnp.broadcast_to(values[:, None], (n_freq, 2, slots)).reshape(count, 1)

    (u0, send) = step(field, -1.0, by_slot=True)
    sent0 = exchange(send, "freq")
    (send,) = step(
        sent0, 1.0, earlier=(u0,), products=((0, 0), (1, 1)), weight=weight, keep=False
    )
    sent = exchange(send, "freq")
    flat = total(total(freq_sums(sent, 2).reshape(-1), "sy"), "sx")
    gamma0, delta0 = flat.reshape(2, n_freq, slots)
    scale = to_rows(gamma0 / delta0)
    u1, send = step(sent, -1.0, earlier=(u0,), scale=scale)
    sent1 = exchange(send, "freq")
    (send,) = step(sent1, 1.0, keep=False)
    u2, send = step(exchange(send, "freq"), -1.0, earlier=(u1,), scale=scale)
    sent2 = exchange(send, "freq")
    (send,) = step(sent2, 1.0, keep=False)
    keys = ((0, 1), (0, 2), (0, 3), (1, 1), (1, 2), (1, 3), (2, 2), (2, 3), (3, 3))
    at = {2: 0, 0: 1, 1: 2, 3: 3}
    (send,) = step(
        exchange(send, "freq"), -1.0, earlier=(u2, u0, u1), scale=scale,
        products=tuple((at[i], at[j]) for i, j in keys), weight=weight, keep=False,
    )
    sent3 = exchange(send, "freq")
    local, *face_vals = apply_local(sent3, pair, omega_rows, odd, 1.0, faces, sides=True)
    (sums,) = finish(
        local, pass_faces(face_vals), odd, n_freq, faces, products=((0, 0),), weight=weight_once,
        keep=False, send=False,
    )
    sums = jnp.sum(exchange(by_slots(sums, 1)[0], "freq"), axis=0)
    others = lax.dynamic_index_in_dim(freq_sums(sent3, len(keys)), me, 1, keepdims=False)
    sums = jnp.concatenate([others, sums[None]], axis=0).reshape(-1)
    sums = total(total(sums, "sy"), "sx").reshape(len(keys) + 1, slots)
    own_gamma = lax.dynamic_index_in_dim(gamma0, me, 0, keepdims=False)
    own_delta = lax.dynamic_index_in_dim(delta0, me, 0, keepdims=False)
    theta = own_delta / own_gamma
    g = {key: sums[k] for k, key in enumerate(keys)}
    g[(0, 0)] = own_gamma
    w = {
        (i, j): theta * (g[(i, j)] - g[(min(i + 1, j), max(i + 1, j))])
        for i in range(3)
        for j in range(i, 4)
    }
    w[(0, 0)] = own_delta
    w[(3, 3)] = sums[len(keys)]
    answer, gamma = solve(theta, g, w)
    residual_level = jnp.log(gamma / float(n_sub * 2 * order))

    adjoint = 0.0
    for values, sent in zip(answer, (sent0, sent1, sent2, sent3)):
        block = lax.dynamic_slice_in_dim(sent, me * own, own, axis=1).astype(F32)
        adjoint = adjoint + block * jnp.tile(values, 2)[None, :, None]
    adjoint = adjoint.reshape(n_freq, 2, slots, faces, run)
    adjoint = jnp.transpose(adjoint, (2, 1, 3, 0, 4)).reshape(slots, 2, faces, face_len)

    state = forward_state[0, 0].astype(F32)
    adj_real, adj_imag = adjoint[:, 0], adjoint[:, 1]
    state_real, state_imag = state[:, 0], state[:, 1]
    term = (
        adj_real * state_real
        - adj_imag * state_imag
        - LOSS_FACTOR * (adj_real * state_imag + adj_imag * state_real)
    )
    dof_total = jnp.sum(term, axis=0).reshape(1, order)
    owner = owner_index[0, 0].reshape(1, order)
    high = jnp.arange(DE_SUB // LOW, dtype=jnp.int32)[:, None]
    low = jnp.arange(LOW, dtype=jnp.int32)[:, None]
    spread = jnp.where(lax.div(owner, LOW) == high, dof_total, 0.0)
    places = jnp.where(lax.rem(owner, LOW) == low, 1.0, 0.0)
    partial_grad = lax.dot_general(
        spread, places, (((1,), (1,)), ((), ())), precision=lax.Precision.HIGHEST
    )
    grad_factor = (DE_SUB / (slots * n_freq * order)) ** 0.5
    partial_grad = (-grad_factor * partial_grad).reshape(n_freq, DE_SUB // n_freq)
    gradient = jnp.sum(exchange(partial_grad, "freq"), axis=0)
    return (adjoint[None, None], gradient[None, None], residual_level)


def solution(mesh):
    return jax.shard_map(
        body,
        mesh=mesh,
        in_specs=(
            P("sx", "sy", None, "freq"),
            P("sx", "sy", None, "freq"),
            P(),
            P("freq"),
            P("sx", "sy", "freq", None, None, None),
            P("sx", "sy", "freq", None, None, None),
            P("sx", "sy", None, None),
        ),
        out_specs=(P("sx", "sy", "freq", None, None, None), P("sx", "sy", "freq"), P("freq")),
        check_vma=False,
    )
```

```python
import functools

import jax
import jax.numpy as jnp
from jax import lax
from jax.experimental import pallas as pl
from jax.experimental.pallas import tpu as pltpu
from jax.sharding import PartitionSpec as P

DE_SUB = 1728
LOSS_FACTOR = 0.3
LOW = 64
BF = jnp.bfloat16
F32 = jnp.float32


def params():
    return pltpu.CompilerParams(vmem_limit_bytes=24 * 1024 * 1024)


def arrange_kernel(stiff_ref, mass_ref, out_ref, order_ref):
    faces, _, run, width = stiff_ref.shape

    @pl.when(pl.program_id(0) == 0)
    def _():
        source = lax.broadcasted_iota(jnp.int32, (width, width), 0)
        target = lax.broadcasted_iota(jnp.int32, (width, width), 1)
        wanted = faces * lax.rem(target, run) + lax.div(target, run)
        order_ref[...] = jnp.where(source == wanted, 1.0, 0.0).astype(BF)

    for at, ref in enumerate((stiff_ref, mass_ref)):
        rows = ref[...].reshape(faces * run, width)
        moved = jnp.dot(rows, order_ref[...], preferred_element_type=F32)
        out_ref[:, at * width : (at + 1) * width] = moved.astype(BF)


def arrange(stiffness, mass_matrix, faces, n_freq, first, count):
    order, width = stiffness.shape
    run = order // (faces * n_freq)
    block = pl.BlockSpec((faces, 1, run, width), lambda d: (0, first + d, 0, 0))
    return pl.pallas_call(
        arrange_kernel,
        grid=(count,),
        in_specs=[block, block],
        out_specs=pl.BlockSpec((width, 2 * width), lambda d: (d, 0)),
        out_shape=jax.ShapeDtypeStruct((count * width, 2 * width), BF),
        scratch_shapes=[pltpu.VMEM((width, width), BF)],
        compiler_params=params(),
        name="arrange",
    )(
        stiffness.reshape(faces, n_freq, run, width),
        mass_matrix.reshape(faces, n_freq, run, width),
    )


def odd_masks(odd_ref, shape):
    return [jnp.broadcast_to(odd_ref[i : i + 1, : shape[1]], shape) > 0.5 for i in range(2)]


def apply_kernel(sign, faces, by_slot, sides, *refs):
    field_ref, near_ref, far_ref, omega_ref, odd_ref, local_ref = refs[:6]
    face_refs = refs[6:-2]
    held_ref, sems = refs[-2:]
    count, width = local_ref.shape
    half = near_ref.shape[0] // width
    block = min(2, half)
    copies = []
    for at in range(0, half, block):
        rows = pl.ds(at * width, block * width)
        copies.append(pltpu.make_async_copy(far_ref.at[rows], held_ref.at[rows], sems.at[at]))
        copies[-1].start()

    def rows_of(first):
        if by_slot:
            taken = field_ref[:, :, first * width : (first + block) * width]
            return taken.reshape(count, block * width)
        return jnp.concatenate([field_ref[first + k, :count, :] for k in range(block)], axis=1)

    result = None
    for first in range(0, 2 * half, block):
        ref, at = (near_ref, first) if first < half else (held_ref, first - half)
        if first >= half:
            copies[at // block].wait()
        part = jnp.dot(
            rows_of(first),
            ref[at * width : (at + block) * width, :],
            preferred_element_type=F32,
        )
        result = part if result is None else result + part
    stiff_part = result[:, :width]
    mass_part = result[:, width:]
    row = lax.broadcasted_iota(jnp.int32, (count, width), 0)
    real = lax.rem(row, 8) < 4
    other = jnp.where(
        real, -pltpu.roll(stiff_part, count - 4, 0), pltpu.roll(stiff_part, 4, 0)
    )
    local = stiff_part + (sign * LOSS_FACTOR) * other - omega_ref[...] * mass_part
    local_ref[...] = local
    run = width // faces
    west, east, south, north = (local[:, f * run : (f + 1) * run] for f in range(faces))
    if sides:
        face_refs[0][...] = east
        face_refs[1][...] = north
        return
    odd_x, odd_y = odd_masks(odd_ref, west.shape)
    face_refs[0][...] = jnp.where(odd_x, west, east)
    face_refs[1][...] = jnp.where(odd_x, east, west)
    face_refs[2][...] = jnp.where(odd_y, south, north)
    face_refs[3][...] = jnp.where(odd_y, north, south)


def apply_local(field, pair, omega_rows, odd, sign, faces, by_slot=False, sides=False):
    length, double = pair[0].shape
    width = double // 2
    count = omega_rows.shape[0]
    run = width // faces
    n_out = 2 if sides else faces
    vmem = pl.BlockSpec(memory_space=pltpu.VMEM)
    return pl.pallas_call(
        functools.partial(apply_kernel, sign, faces, by_slot, sides),
        in_specs=[
            vmem,
            vmem,
            pl.BlockSpec(memory_space=pltpu.HBM),
            vmem,
            vmem,
        ],
        out_specs=[vmem] * (1 + n_out),
        out_shape=[jax.ShapeDtypeStruct((count, width), F32)]
        + [jax.ShapeDtypeStruct((count, run), F32)] * n_out,
        scratch_shapes=[
            pltpu.VMEM((length, double), BF),
            pltpu.SemaphoreType.DMA((length // width,)),
        ],
        compiler_params=params(),
        name="apply_local",
    )(field, *pair, omega_rows, odd)


def permute(values, axis, pairs):
    return lax.ppermute(values, axis, pairs) if pairs else jnp.zeros_like(values)


def swap_faces(face_vals):
    out = {}
    for axis, (near, far) in (("sx", face_vals[:2]), ("sy", face_vals[2:])):
        count = lax.axis_size(axis)
        low = [(i, i ^ 1) for i in range(count)]
        high = [(i, ((i + 1) ^ 1) - 1) for i in range(1, count - 1)]
        with jax.named_scope("halo_" + axis):
            out[axis] = [permute(near, axis, low), permute(far, axis, high)]
    return out["sx"] + out["sy"]


def pass_faces(face_vals):
    out = []
    for axis, values in zip(("sx", "sy"), face_vals):
        pairs = [(i, i + 1) for i in range(lax.axis_size(axis) - 1)]
        out.append(permute(values, axis, pairs))
    return out


def finish_kernel(plan, faces, n_in, copies, *refs):
    combine, products, keep, send, n_halo = plan
    odd_ref, local_ref = refs[:2]
    halo = [ref[...] for ref in refs[2 : 2 + n_halo]]
    at = 2 + n_halo
    earlier = refs[at : at + n_in]
    at += n_in
    coefs_ref = weight_ref = None
    if combine:
        coefs_ref, at = refs[at], at + 1
    if products:
        weight_ref, at = refs[at], at + 1
    outs = list(refs[at:])
    if n_halo == faces:
        near_x, far_x, near_y, far_y = halo
        odd_x, odd_y = odd_masks(odd_ref, near_x.shape)
        halo = [
            jnp.where(odd_x, near_x, far_x),
            jnp.where(odd_x, far_x, near_x),
            jnp.where(odd_y, near_y, far_y),
            jnp.where(odd_y, far_y, near_y),
        ]
    else:
        none = jnp.zeros_like(halo[0])
        halo = [halo[0], none, halo[1], none]
    vector = local_ref[...] + jnp.concatenate(halo, axis=1)
    count, width = vector.shape
    known = [ref[...] for ref in earlier]
    if combine:
        vector = known[0] - coefs_ref[...] * vector
    known.append(vector)
    if keep:
        outs.pop(0)[...] = vector
    sums = None
    if products:
        weighted = {left: known[left] * weight_ref[...] for left, _ in products}
        ones = jnp.ones((8, 128), F32)
        high = -(-len(products) // 8) * 8
        place = lax.broadcasted_iota(jnp.int32, (high, count), 0)
        sums = jnp.zeros((high, count), F32)
        for slot, (left, right) in enumerate(products):
            value = weighted[left] * known[right]
            value = sum(value[:, k : k + 128] for k in range(0, width, 128))
            value = lax.dot_general(
                ones,
                value,
                (((1,), (1,)), ((), ())),
                precision=lax.Precision.HIGHEST,
                preferred_element_type=F32,
            )
            sums = jnp.where(place == slot, value[:1], sums)
    if send:
        sent = vector.astype(BF)
        out = outs.pop(0)
        extra = None
        if products:
            parts = []
            for _ in range(3):
                part = sums.astype(BF)
                parts.append(part.astype(F32))
                sums = sums - parts[-1]
            parts.append(jnp.zeros((sums.shape[0], width - 3 * count), F32))
            extra = jnp.concatenate(parts, axis=1).astype(BF)
        for copy in range(copies):
            out[copy, :count, :] = sent
            if extra is not None:
                out[copy, count:, :] = extra
    elif products:
        outs.pop(0)[...] = sums


def finish(
    local, halos, odd, n_freq, faces, earlier=(), scale=None, products=(),
    weight=None, keep=True, send=True,
):
    count, width = local.shape
    args = [odd, local, *halos, *earlier]
    if scale is not None:
        args.append(scale)
    if products:
        args.append(weight)
    shapes = []
    high = -(-len(products) // 8) * 8
    if keep:
        shapes.append(jax.ShapeDtypeStruct((count, width), F32))
    if send:
        shapes.append(jax.ShapeDtypeStruct((n_freq, count + high, width), BF))
    elif products:
        shapes.append(jax.ShapeDtypeStruct((high, count), F32))
    plan = (scale is not None, tuple(products), keep, send, len(halos))
    vmem = pl.BlockSpec(memory_space=pltpu.VMEM)
    return pl.pallas_call(
        functools.partial(finish_kernel, plan, faces, len(earlier), n_freq),
        in_specs=[vmem] * len(args),
        out_specs=[vmem] * len(shapes),
        out_shape=shapes,
        compiler_params=params(),
        name="finish",
    )(*args)


def exchange(blocks, axis):
    return lax.all_to_all(blocks, axis, 0, 0, tiled=False)


def total(values, axis):
    count = lax.axis_size(axis)
    return jnp.sum(exchange(jnp.broadcast_to(values[None], (count, *values.shape)), axis), axis=0)


def quad(entries, coefs):
    result = 0.0
    for i, left in enumerate(coefs):
        for j in range(i, len(coefs)):
            if left is None or coefs[j] is None:
                continue
            term = left * coefs[j] * entries[(i, j)]
            result = result + (term if i == j else 2.0 * term)
    return result


def combo(first, scale, second):
    out = []
    for a, b in zip(first, second):
        b = None if b is None else scale * b
        out.append(b if a is None else a if b is None else a + b)
    return out


def solve(theta, g, w):
    one = jnp.ones_like(theta)
    residual = direction = [one, None, None, None]
    answer = [None] * 4
    gamma = quad(g, residual)
    for iteration in range(4):
        alpha = gamma / quad(w, direction)
        answer = combo(answer, alpha, direction)
        if iteration < 3:
            below = [None] + direction[:3]
            image = combo([None if c is None else theta * c for c in direction], -theta, below)
            residual = combo(residual, -alpha, image)
            gamma_next = quad(g, residual)
            direction = combo(residual, gamma_next / gamma, direction)
            gamma = gamma_next
    return answer, gamma


def body(stiffness, mass_matrix, omega_table, assignment, adjoint_load, forward_state, owner_index):
    n_freq = lax.axis_size("freq")
    n_sub = lax.axis_size("sx") * lax.axis_size("sy")
    slots, faces, face_len = adjoint_load.shape[2], adjoint_load.shape[4], adjoint_load.shape[5]
    order = faces * face_len
    run = face_len // n_freq
    width = faces * run
    count = n_freq * slots * 2
    own = 2 * slots
    me = lax.axis_index("freq")

    load = jnp.swapaxes(adjoint_load[0, 0].astype(BF), 0, 1).reshape(own, faces, n_freq, run)
    load = jnp.swapaxes(load, 1, 2).reshape(own, order)
    tags = jnp.broadcast_to(assignment.astype(BF)[None, :], (2, slots)).reshape(own, 1)
    packet = jnp.concatenate([load, jnp.broadcast_to(tags, (own, 128))], axis=1)
    field = exchange(jnp.broadcast_to(packet[None], (n_freq, *packet.shape)), "freq")
    half = n_freq // 2
    pair = tuple(
        pltpu.with_memory_space_constraint(
            arrange(stiffness[0, 0], mass_matrix[0, 0], faces, n_freq, first, half), place
        )
        for first, place in ((0, pltpu.VMEM), (half, pltpu.HBM))
    )
    slot_tags = field[:, :, order].reshape(count).astype(jnp.int32)
    matches = slot_tags[:, None] == jnp.arange(omega_table.shape[0], dtype=jnp.int32)[None, :]
    omega_rows = jnp.sum(jnp.where(matches, omega_table[None, :], 0.0), axis=1, keepdims=True)

    def inside(axis, at):
        return jnp.where(lax.axis_index(axis) == at, 1.0, 0.5).astype(F32)

    face_weight = jnp.stack(
        [
            inside("sx", 0),
            inside("sx", lax.axis_size("sx") - 1),
            inside("sy", 0),
            inside("sy", lax.axis_size("sy") - 1),
        ]
    )
    weight = jnp.repeat(face_weight, run)[None, :]
    once = jnp.where(face_weight < 1.0, jnp.array([1.0, 0.0, 1.0, 0.0], F32), 1.0)
    weight_once = jnp.repeat(once, run)[None, :]

    odd = jnp.stack([lax.rem(lax.axis_index(axis), 2) for axis in ("sx", "sy")]).astype(F32)
    odd = jnp.broadcast_to(odd[:, None], (2, 128))

    def step(field, sign, by_slot=False, **how):
        local, *face_vals = apply_local(field, pair, omega_rows, odd, sign, faces, by_slot)
        return finish(local, swap_faces(face_vals), odd, n_freq, faces, **how)

    def by_slots(sums, n_products):
        return jnp.sum(sums[:n_products].reshape(n_products, n_freq, 2, slots), axis=2)

    def freq_sums(sent, n_products):
        sums = sum(
            jnp.sum(sent[:, count:, k * count : (k + 1) * count].astype(F32), axis=0)
            for k in range(3)
        )
        return by_slots(sums, n_products)

    def to_rows(values):
        return jnp.broadcast_to(values[:, None], (n_freq, 2, slots)).reshape(count, 1)

    (u0, send) = step(field, -1.0, by_slot=True)
    sent0 = exchange(send, "freq")
    (send,) = step(
        sent0, 1.0, earlier=(u0,), products=((0, 0), (1, 1)), weight=weight, keep=False
    )
    sent = exchange(send, "freq")
    flat = total(total(freq_sums(sent, 2).reshape(-1), "sy"), "sx")
    gamma0, delta0 = flat.reshape(2, n_freq, slots)
    scale = to_rows(gamma0 / delta0)
    u1, send = step(sent, -1.0, earlier=(u0,), scale=scale)
    sent1 = exchange(send, "freq")
    (send,) = step(sent1, 1.0, keep=False)
    u2, send = step(exchange(send, "freq"), -1.0, earlier=(u1,), scale=scale)
    sent2 = exchange(send, "freq")
    (send,) = step(sent2, 1.0, keep=False)
    keys = ((0, 1), (0, 2), (0, 3), (1, 1), (1, 2), (1, 3), (2, 2), (2, 3), (3, 3))
    at = {2: 0, 0: 1, 1: 2, 3: 3}
    (send,) = step(
        exchange(send, "freq"), -1.0, earlier=(u2, u0, u1), scale=scale,
        products=tuple((at[i], at[j]) for i, j in keys), weight=weight, keep=False,
    )
    sent3 = exchange(send, "freq")
    local, *face_vals = apply_local(sent3, pair, omega_rows, odd, 1.0, faces, sides=True)
    (sums,) = finish(
        local, pass_faces(face_vals), odd, n_freq, faces, products=((0, 0),), weight=weight_once,
        keep=False, send=False,
    )
    sums = jnp.concatenate([freq_sums(sent3, len(keys)) / n_freq, by_slots(sums, 1)], axis=0)
    sums = jnp.swapaxes(sums, 0, 1).reshape(n_freq, 1, (len(keys) + 1) * slots)
    size_y = lax.axis_size("sy")
    sums = jnp.broadcast_to(sums, (n_freq, size_y, sums.shape[2]))
    sums = sums.reshape(n_freq * size_y, sums.shape[2])
    sums = jnp.sum(exchange(sums, ("freq", "sy")), axis=0)
    sums = total(sums, "sx").reshape(len(keys) + 1, slots)
    own_gamma = lax.dynamic_index_in_dim(gamma0, me, 0, keepdims=False)
    own_delta = lax.dynamic_index_in_dim(delta0, me, 0, keepdims=False)
    theta = own_delta / own_gamma
    g = {key: sums[k] for k, key in enumerate(keys)}
    g[(0, 0)] = own_gamma
    w = {
        (i, j): theta * (g[(i, j)] - g[(min(i + 1, j), max(i + 1, j))])
        for i in range(3)
        for j in range(i, 4)
    }
    w[(0, 0)] = own_delta
    w[(3, 3)] = sums[len(keys)]
    answer, gamma = solve(theta, g, w)
    residual_level = jnp.log(gamma / float(n_sub * 2 * order))

    adjoint = 0.0
    for values, sent in zip(answer, (sent0, sent1, sent2, sent3)):
        block = lax.dynamic_slice_in_dim(sent, me * own, own, axis=1).astype(F32)
        adjoint = adjoint + block * jnp.tile(values, 2)[None, :, None]
    adjoint = adjoint.reshape(n_freq, 2, slots, faces, run)
    adjoint = jnp.transpose(adjoint, (2, 1, 3, 0, 4)).reshape(slots, 2, faces, face_len)

    state = forward_state[0, 0].astype(F32)
    adj_real, adj_imag = adjoint[:, 0], adjoint[:, 1]
    state_real, state_imag = state[:, 0], state[:, 1]
    term = (
        adj_real * state_real
        - adj_imag * state_imag
        - LOSS_FACTOR * (adj_real * state_imag + adj_imag * state_real)
    )
    dof_total = jnp.sum(term, axis=0).reshape(1, order)
    owner = owner_index[0, 0].reshape(1, order)
    high = jnp.arange(DE_SUB // LOW, dtype=jnp.int32)[:, None]
    low = jnp.arange(LOW, dtype=jnp.int32)[:, None]
    spread = jnp.where(lax.div(owner, LOW) == high, dof_total, 0.0)
    places = jnp.where(lax.rem(owner, LOW) == low, 1.0, 0.0)
    partial_grad = lax.dot_general(
        spread, places, (((1,), (1,)), ((), ())), precision=lax.Precision.HIGHEST
    )
    grad_factor = (DE_SUB / (slots * n_freq * order)) ** 0.5
    partial_grad = (-grad_factor * partial_grad).reshape(n_freq, DE_SUB // n_freq)
    gradient = jnp.sum(exchange(partial_grad, "freq"), axis=0)
    return (adjoint[None, None], gradient[None, None], residual_level)


def solution(mesh):
    return jax.shard_map(
        body,
        mesh=mesh,
        in_specs=(
            P("sx", "sy", None, "freq"),
            P("sx", "sy", None, "freq"),
            P(),
            P("freq"),
            P("sx", "sy", "freq", None, None, None),
            P("sx", "sy", "freq", None, None, None),
            P("sx", "sy", None, None),
        ),
        out_specs=(P("sx", "sy", "freq", None, None, None), P("sx", "sy", "freq"), P("freq")),
        check_vma=False,
    )
```

```python
import functools

import jax
import jax.numpy as jnp
from jax import lax
from jax.experimental import pallas as pl
from jax.experimental.pallas import tpu as pltpu
from jax.sharding import PartitionSpec as P

DE_SUB = 1728
LOSS_FACTOR = 0.3
LOW = 64
BF = jnp.bfloat16
F32 = jnp.float32


def params():
    return pltpu.CompilerParams(vmem_limit_bytes=24 * 1024 * 1024)


def arrange_kernel(stiff_ref, mass_ref, out_ref, order_ref):
    faces, _, run, width = stiff_ref.shape

    @pl.when(pl.program_id(0) == 0)
    def _():
        source = lax.broadcasted_iota(jnp.int32, (width, width), 0)
        target = lax.broadcasted_iota(jnp.int32, (width, width), 1)
        wanted = faces * lax.rem(target, run) + lax.div(target, run)
        order_ref[...] = jnp.where(source == wanted, 1.0, 0.0).astype(BF)

    for at, ref in enumerate((stiff_ref, mass_ref)):
        rows = ref[...].reshape(faces * run, width)
        moved = jnp.dot(rows, order_ref[...], preferred_element_type=F32)
        out_ref[:, at * width : (at + 1) * width] = moved.astype(BF)


def arrange(stiffness, mass_matrix, faces, n_freq, first, count):
    order, width = stiffness.shape
    run = order // (faces * n_freq)
    block = pl.BlockSpec((faces, 1, run, width), lambda d: (0, first + d, 0, 0))
    return pl.pallas_call(
        arrange_kernel,
        grid=(count,),
        in_specs=[block, block],
        out_specs=pl.BlockSpec((width, 2 * width), lambda d: (d, 0)),
        out_shape=jax.ShapeDtypeStruct((count * width, 2 * width), BF),
        scratch_shapes=[pltpu.VMEM((width, width), BF)],
        compiler_params=params(),
        name="arrange",
    )(
        *(
            pltpu.with_memory_space_constraint(matrix.reshape(faces, n_freq, run, width), pltpu.HBM)
            for matrix in (stiffness, mass_matrix)
        )
    )


def packet_kernel(load_ref, tags_ref, out_ref):
    slots, parts, faces, length = load_ref.shape
    n_freq = out_ref.shape[0]
    run = length // n_freq
    by_face = [
        jnp.concatenate(
            [load_ref[k, p, f : f + 1, :] for p in range(parts) for k in range(slots)], axis=0
        )
        for f in range(faces)
    ]
    pieces = [
        by_face[f][:, d * run : (d + 1) * run] for d in range(n_freq) for f in range(faces)
    ]
    packet = jnp.concatenate(pieces + [tags_ref[...]], axis=1).astype(BF)
    for d in range(n_freq):
        out_ref[d] = packet


def packet_of(load, tags, n_freq):
    slots, parts, faces, length = load.shape
    own = slots * parts
    vmem = pl.BlockSpec(memory_space=pltpu.VMEM)
    return pl.pallas_call(
        packet_kernel,
        in_specs=[vmem, vmem],
        out_specs=vmem,
        out_shape=jax.ShapeDtypeStruct((n_freq, own, faces * length + 128), BF),
        compiler_params=params(),
        name="packet",
    )(load, tags)


def odd_masks(odd_ref, shape):
    return [jnp.broadcast_to(odd_ref[i : i + 1, : shape[1]], shape) > 0.5 for i in range(2)]


def apply_kernel(sign, faces, by_slot, sides, *refs):
    field_ref, near_ref, far_ref, omega_ref, odd_ref, local_ref = refs[:6]
    face_refs = refs[6:-2]
    held_ref, sems = refs[-2:]
    count, width = local_ref.shape
    half = near_ref.shape[0] // width
    block = min(2, half)
    copies = []
    for at in range(0, half, block):
        rows = pl.ds(at * width, block * width)
        copies.append(pltpu.make_async_copy(far_ref.at[rows], held_ref.at[rows], sems.at[at]))
        copies[-1].start()

    def rows_of(first):
        if by_slot:
            taken = field_ref[:, :, first * width : (first + block) * width]
            return taken.reshape(count, block * width)
        return jnp.concatenate([field_ref[first + k, :count, :] for k in range(block)], axis=1)

    result = None
    for first in range(0, 2 * half, block):
        ref, at = (near_ref, first) if first < half else (held_ref, first - half)
        if first >= half:
            copies[at // block].wait()
        part = jnp.dot(
            rows_of(first),
            ref[at * width : (at + block) * width, :],
            preferred_element_type=F32,
        )
        result = part if result is None else result + part
    stiff_part = result[:, :width]
    mass_part = result[:, width:]
    row = lax.broadcasted_iota(jnp.int32, (count, width), 0)
    real = lax.rem(row, 8) < 4
    other = jnp.where(
        real, -pltpu.roll(stiff_part, count - 4, 0), pltpu.roll(stiff_part, 4, 0)
    )
    local = stiff_part + (sign * LOSS_FACTOR) * other - omega_ref[...] * mass_part
    local_ref[...] = local
    run = width // faces
    west, east, south, north = (local[:, f * run : (f + 1) * run] for f in range(faces))
    if sides:
        face_refs[0][...] = east
        face_refs[1][...] = north
        return
    odd_x, odd_y = odd_masks(odd_ref, west.shape)
    face_refs[0][...] = jnp.where(odd_x, west, east)
    face_refs[1][...] = jnp.where(odd_x, east, west)
    face_refs[2][...] = jnp.where(odd_y, south, north)
    face_refs[3][...] = jnp.where(odd_y, north, south)


def apply_local(field, pair, omega_rows, odd, sign, faces, by_slot=False, sides=False):
    length, double = pair[0].shape
    width = double // 2
    count = omega_rows.shape[0]
    run = width // faces
    n_out = 2 if sides else faces
    vmem = pl.BlockSpec(memory_space=pltpu.VMEM)
    return pl.pallas_call(
        functools.partial(apply_kernel, sign, faces, by_slot, sides),
        in_specs=[
            vmem,
            vmem,
            pl.BlockSpec(memory_space=pltpu.HBM),
            vmem,
            vmem,
        ],
        out_specs=[vmem] * (1 + n_out),
        out_shape=[jax.ShapeDtypeStruct((count, width), F32)]
        + [jax.ShapeDtypeStruct((count, run), F32)] * n_out,
        scratch_shapes=[
            pltpu.VMEM((length, double), BF),
            pltpu.SemaphoreType.DMA((length // width,)),
        ],
        compiler_params=params(),
        name="apply_local",
    )(field, *pair, omega_rows, odd)


def permute(values, axis, pairs):
    return lax.ppermute(values, axis, pairs) if pairs else jnp.zeros_like(values)


def swap_faces(face_vals):
    out = {}
    for axis, (near, far) in (("sx", face_vals[:2]), ("sy", face_vals[2:])):
        count = lax.axis_size(axis)
        low = [(i, i ^ 1) for i in range(count)]
        high = [(i, ((i + 1) ^ 1) - 1) for i in range(1, count - 1)]
        with jax.named_scope("halo_" + axis):
            out[axis] = [permute(near, axis, low), permute(far, axis, high)]
    return out["sx"] + out["sy"]


def pass_faces(face_vals):
    out = []
    for axis, values in zip(("sx", "sy"), face_vals):
        pairs = [(i, i + 1) for i in range(lax.axis_size(axis) - 1)]
        out.append(permute(values, axis, pairs))
    return out


def finish_kernel(plan, faces, n_in, copies, *refs):
    combine, products, keep, send, n_halo = plan
    odd_ref, local_ref = refs[:2]
    halo = [ref[...] for ref in refs[2 : 2 + n_halo]]
    at = 2 + n_halo
    earlier = refs[at : at + n_in]
    at += n_in
    coefs_ref = weight_ref = None
    if combine:
        coefs_ref, at = refs[at], at + 1
    if products:
        weight_ref, at = refs[at], at + 1
    outs = list(refs[at:])
    if n_halo == faces:
        near_x, far_x, near_y, far_y = halo
        odd_x, odd_y = odd_masks(odd_ref, near_x.shape)
        halo = [
            jnp.where(odd_x, near_x, far_x),
            jnp.where(odd_x, far_x, near_x),
            jnp.where(odd_y, near_y, far_y),
            jnp.where(odd_y, far_y, near_y),
        ]
    else:
        none = jnp.zeros_like(halo[0])
        halo = [halo[0], none, halo[1], none]
    vector = local_ref[...] + jnp.concatenate(halo, axis=1)
    count, width = vector.shape
    known = [ref[...] for ref in earlier]
    if combine:
        vector = known[0] - coefs_ref[...] * vector
    known.append(vector)
    if keep:
        outs.pop(0)[...] = vector
    sums = None
    if products:
        weighted = {left: known[left] * weight_ref[...] for left, _ in products}
        ones = jnp.ones((8, 128), F32)
        high = -(-len(products) // 8) * 8
        place = lax.broadcasted_iota(jnp.int32, (high, count), 0)
        sums = jnp.zeros((high, count), F32)
        for slot, (left, right) in enumerate(products):
            value = weighted[left] * known[right]
            value = sum(value[:, k : k + 128] for k in range(0, width, 128))
            value = lax.dot_general(
                ones,
                value,
                (((1,), (1,)), ((), ())),
                precision=lax.Precision.HIGHEST,
                preferred_element_type=F32,
            )
            sums = jnp.where(place == slot, value[:1], sums)
    if send:
        sent = vector.astype(BF)
        out = outs.pop(0)
        extra = None
        if products:
            parts = []
            for _ in range(3):
                part = sums.astype(BF)
                parts.append(part.astype(F32))
                sums = sums - parts[-1]
            parts.append(jnp.zeros((sums.shape[0], width - 3 * count), F32))
            extra = jnp.concatenate(parts, axis=1).astype(BF)
        for copy in range(copies):
            out[copy, :count, :] = sent
            if extra is not None:
                out[copy, count:, :] = extra
    elif products:
        outs.pop(0)[...] = sums


def finish(
    local, halos, odd, n_freq, faces, earlier=(), scale=None, products=(),
    weight=None, keep=True, send=True,
):
    count, width = local.shape
    args = [odd, local, *halos, *earlier]
    if scale is not None:
        args.append(scale)
    if products:
        args.append(weight)
    shapes = []
    high = -(-len(products) // 8) * 8
    if keep:
        shapes.append(jax.ShapeDtypeStruct((count, width), F32))
    if send:
        shapes.append(jax.ShapeDtypeStruct((n_freq, count + high, width), BF))
    elif products:
        shapes.append(jax.ShapeDtypeStruct((high, count), F32))
    plan = (scale is not None, tuple(products), keep, send, len(halos))
    vmem = pl.BlockSpec(memory_space=pltpu.VMEM)
    return pl.pallas_call(
        functools.partial(finish_kernel, plan, faces, len(earlier), n_freq),
        in_specs=[vmem] * len(args),
        out_specs=[vmem] * len(shapes),
        out_shape=shapes,
        compiler_params=params(),
        name="finish",
    )(*args)


def exchange(blocks, axis):
    return lax.all_to_all(blocks, axis, 0, 0, tiled=False)


def total(values, axis):
    count = lax.axis_size(axis)
    return jnp.sum(exchange(jnp.broadcast_to(values[None], (count, *values.shape)), axis), axis=0)


def quad(entries, coefs):
    result = 0.0
    for i, left in enumerate(coefs):
        for j in range(i, len(coefs)):
            if left is None or coefs[j] is None:
                continue
            term = left * coefs[j] * entries[(i, j)]
            result = result + (term if i == j else 2.0 * term)
    return result


def combo(first, scale, second):
    out = []
    for a, b in zip(first, second):
        b = None if b is None else scale * b
        out.append(b if a is None else a if b is None else a + b)
    return out


def solve(theta, g, w):
    one = jnp.ones_like(theta)
    residual = direction = [one, None, None, None]
    answer = [None] * 4
    gamma = quad(g, residual)
    for iteration in range(4):
        alpha = gamma / quad(w, direction)
        answer = combo(answer, alpha, direction)
        if iteration < 3:
            below = [None] + direction[:3]
            image = combo([None if c is None else theta * c for c in direction], -theta, below)
            residual = combo(residual, -alpha, image)
            gamma_next = quad(g, residual)
            direction = combo(residual, gamma_next / gamma, direction)
            gamma = gamma_next
    return answer, gamma


def body(stiffness, mass_matrix, omega_table, assignment, adjoint_load, forward_state, owner_index):
    n_freq = lax.axis_size("freq")
    n_sub = lax.axis_size("sx") * lax.axis_size("sy")
    slots, faces, face_len = adjoint_load.shape[2], adjoint_load.shape[4], adjoint_load.shape[5]
    order = faces * face_len
    run = face_len // n_freq
    width = faces * run
    count = n_freq * slots * 2
    own = 2 * slots
    me = lax.axis_index("freq")

    tags = jnp.broadcast_to(assignment.astype(F32)[None, :], (2, slots)).reshape(own, 1)
    packet = packet_of(adjoint_load[0, 0], jnp.broadcast_to(tags, (own, 128)), n_freq)
    field = exchange(packet, "freq")
    half = n_freq // 2
    pair = tuple(
        pltpu.with_memory_space_constraint(
            arrange(stiffness[0, 0], mass_matrix[0, 0], faces, n_freq, first, half), place
        )
        for first, place in ((0, pltpu.VMEM), (half, pltpu.HBM))
    )
    slot_tags = field[:, :, order].reshape(count).astype(jnp.int32)
    matches = slot_tags[:, None] == jnp.arange(omega_table.shape[0], dtype=jnp.int32)[None, :]
    omega_rows = jnp.sum(jnp.where(matches, omega_table[None, :], 0.0), axis=1, keepdims=True)

    def inside(axis, at):
        return jnp.where(lax.axis_index(axis) == at, 1.0, 0.5).astype(F32)

    face_weight = jnp.stack(
        [
            inside("sx", 0),
            inside("sx", lax.axis_size("sx") - 1),
            inside("sy", 0),
            inside("sy", lax.axis_size("sy") - 1),
        ]
    )
    weight = jnp.repeat(face_weight, run)[None, :]
    once = jnp.where(face_weight < 1.0, jnp.array([1.0, 0.0, 1.0, 0.0], F32), 1.0)
    weight_once = jnp.repeat(once, run)[None, :]

    odd = jnp.stack([lax.rem(lax.axis_index(axis), 2) for axis in ("sx", "sy")]).astype(F32)
    odd = jnp.broadcast_to(odd[:, None], (2, 128))

    def step(field, sign, by_slot=False, **how):
        local, *face_vals = apply_local(field, pair, omega_rows, odd, sign, faces, by_slot)
        return finish(local, swap_faces(face_vals), odd, n_freq, faces, **how)

    def by_slots(sums, n_products):
        return jnp.sum(sums[:n_products].reshape(n_products, n_freq, 2, slots), axis=2)

    def freq_sums(sent, n_products):
        sums = sum(
            jnp.sum(sent[:, count:, k * count : (k + 1) * count].astype(F32), axis=0)
            for k in range(3)
        )
        return by_slots(sums, n_products)

    def to_rows(values):
        return jnp.broadcast_to(values[:, None], (n_freq, 2, slots)).reshape(count, 1)

    (u0, send) = step(field, -1.0, by_slot=True)
    sent0 = exchange(send, "freq")
    (send,) = step(
        sent0, 1.0, earlier=(u0,), products=((0, 0), (1, 1)), weight=weight, keep=False
    )
    sent = exchange(send, "freq")
    flat = total(total(freq_sums(sent, 2).reshape(-1), "sy"), "sx")
    gamma0, delta0 = flat.reshape(2, n_freq, slots)
    scale = to_rows(gamma0 / delta0)
    u1, send = step(sent, -1.0, earlier=(u0,), scale=scale)
    sent1 = exchange(send, "freq")
    (send,) = step(sent1, 1.0, keep=False)
    u2, send = step(exchange(send, "freq"), -1.0, earlier=(u1,), scale=scale)
    sent2 = exchange(send, "freq")
    (send,) = step(sent2, 1.0, keep=False)
    keys = ((0, 1), (0, 2), (0, 3), (1, 1), (1, 2), (1, 3), (2, 2), (2, 3), (3, 3))
    at = {2: 0, 0: 1, 1: 2, 3: 3}
    (send,) = step(
        exchange(send, "freq"), -1.0, earlier=(u2, u0, u1), scale=scale,
        products=tuple((at[i], at[j]) for i, j in keys), weight=weight, keep=False,
    )
    sent3 = exchange(send, "freq")
    local, *face_vals = apply_local(sent3, pair, omega_rows, odd, 1.0, faces, sides=True)
    (sums,) = finish(
        local, pass_faces(face_vals), odd, n_freq, faces, products=((0, 0),), weight=weight_once,
        keep=False, send=False,
    )
    sums = jnp.concatenate([freq_sums(sent3, len(keys)) / n_freq, by_slots(sums, 1)], axis=0)
    sums = jnp.swapaxes(sums, 0, 1).reshape(n_freq, 1, (len(keys) + 1) * slots)
    size_y = lax.axis_size("sy")
    sums = jnp.broadcast_to(sums, (n_freq, size_y, sums.shape[2]))
    sums = sums.reshape(n_freq * size_y, sums.shape[2])
    sums = jnp.sum(exchange(sums, ("freq", "sy")), axis=0)
    sums = total(sums, "sx").reshape(len(keys) + 1, slots)
    own_gamma = lax.dynamic_index_in_dim(gamma0, me, 0, keepdims=False)
    own_delta = lax.dynamic_index_in_dim(delta0, me, 0, keepdims=False)
    theta = own_delta / own_gamma
    g = {key: sums[k] for k, key in enumerate(keys)}
    g[(0, 0)] = own_gamma
    w = {
        (i, j): theta * (g[(i, j)] - g[(min(i + 1, j), max(i + 1, j))])
        for i in range(3)
        for j in range(i, 4)
    }
    w[(0, 0)] = own_delta
    w[(3, 3)] = sums[len(keys)]
    answer, gamma = solve(theta, g, w)
    residual_level = jnp.log(gamma / float(n_sub * 2 * order))

    adjoint = 0.0
    for values, sent in zip(answer, (sent0, sent1, sent2, sent3)):
        block = lax.dynamic_slice_in_dim(sent, me * own, own, axis=1).astype(F32)
        adjoint = adjoint + block * jnp.tile(values, 2)[None, :, None]
    adjoint = adjoint.reshape(n_freq, 2, slots, faces, run)
    adjoint = jnp.transpose(adjoint, (2, 1, 3, 0, 4)).reshape(slots, 2, faces, face_len)

    state = forward_state[0, 0].astype(F32)
    adj_real, adj_imag = adjoint[:, 0], adjoint[:, 1]
    state_real, state_imag = state[:, 0], state[:, 1]
    term = (
        adj_real * state_real
        - adj_imag * state_imag
        - LOSS_FACTOR * (adj_real * state_imag + adj_imag * state_real)
    )
    dof_total = jnp.sum(term, axis=0).reshape(1, order)
    owner = owner_index[0, 0].reshape(1, order)
    high = jnp.arange(DE_SUB // LOW, dtype=jnp.int32)[:, None]
    low = jnp.arange(LOW, dtype=jnp.int32)[:, None]
    spread = jnp.where(lax.div(owner, LOW) == high, dof_total, 0.0)
    places = jnp.where(lax.rem(owner, LOW) == low, 1.0, 0.0)
    partial_grad = lax.dot_general(
        spread, places, (((1,), (1,)), ((), ())), precision=lax.Precision.HIGHEST
    )
    grad_factor = (DE_SUB / (slots * n_freq * order)) ** 0.5
    partial_grad = (-grad_factor * partial_grad).reshape(n_freq, DE_SUB // n_freq)
    gradient = jnp.sum(exchange(partial_grad, "freq"), axis=0)
    return (adjoint[None, None], gradient[None, None], residual_level)


def solution(mesh):
    return jax.shard_map(
        body,
        mesh=mesh,
        in_specs=(
            P("sx", "sy", None, "freq"),
            P("sx", "sy", None, "freq"),
            P(),
            P("freq"),
            P("sx", "sy", "freq", None, None, None),
            P("sx", "sy", "freq", None, None, None),
            P("sx", "sy", None, None),
        ),
        out_specs=(P("sx", "sy", "freq", None, None, None), P("sx", "sy", "freq"), P("freq")),
        check_vma=False,
    )
```
